128 devices in a mesh: space: 8 (over x, core), chan: 16 (over z, y).
Axes of the slice: x: 4, y: 4, z: 4, core: 2. Of those that a mesh axis runs over, the one named last changes fastest.
Arguments:
- grid_in: bfloat16 [227, 131072], P(None, ('space', 'chan')), may hold values from -6 to 6
- grid_embed_w: bfloat16 [512, 227], replicated, may hold values from -0.375 to 0.375
- g2m_w: bfloat16 [512, 512], replicated, may hold values from -0.25 to 0.25
- pair_w: bfloat16 [4, 2, 512, 512], replicated, may hold values from -0.25 to 0.25
- second_w: bfloat16 [5, 512, 512], replicated, may hold values from -0.25 to 0.25
- first_b: float32 [6, 512], replicated, may hold values from -4 to 4
- norm_gain: float32 [5, 512], replicated, may hold values from 0.5 to 1.5
- geom_w: bfloat16 [3, 512, 4], replicated, may hold values from -3 to 3
- out_w: bfloat16 [227, 512], replicated, may hold values from -0.25 to 0.25
- out_b: float32 [227], replicated, may hold values from -4 to 4
- g2m_geom: bfloat16 [4, 196608], P(None, ('space', 'chan')), may hold values from -6 to 6
- mesh_geom: bfloat16 [4, 262144], P(None, ('space', 'chan')), may hold values from -6 to 6
- m2g_geom: bfloat16 [4, 393216], P(None, ('space', 'chan')), may hold values from -6 to 6
- g2m_send: int32 [196608], P(('space', 'chan')), may hold values from 0 to 131071, as said below
- g2m_recv: int32 [196608], P(('space', 'chan')), may hold values from 0 to 65535, as said below
- mesh_recv: int32 [262144], P(('space', 'chan')), may hold values from 0 to 65535, as said below
- mesh_slot: int32 [262144], P(('space', 'chan')), may hold values from 0 to 2047
- mesh_rows: int32 [16384, 16], P(('space', 'chan')), may hold values from 0 to 511
- m2g_send: int32 [393216], P(('space', 'chan')), may hold values from 0 to 65535, as said below
Outputs:
- prediction: float32 [227, 131072], P(None, ('space', 'chan'))
- mesh_state: bfloat16 [512, 65536], P(None, ('space', 'chan'))
The draws below stay inside these ranges and needn't reach their ends.
Inputs may be any that keep to these rules, and one draw needn't show every extreme that they name: `g2m_send`: the edges of block d (1536 edges each) send from grid cells d * 1024 - 256 to (d + 1) * 1024 + 255, within the grid. `g2m_recv`: the edges of block d (1536 edges each) end at mesh nodes d * 512 to (d + 1) * 512 - 1. `mesh_recv`: the edges of block d (2048 edges each) end at mesh nodes d * 512 to (d + 1) * 512 - 1. `m2g_send`: for grid cell g in block d = g // 1024, the edges 3g to 3g + 2 send from mesh nodes d * 512 - 128 to (d + 1) * 512 + 127, within the mesh.
All inputs are finite; a program needn't handle non-finite values.
Results may differ from the reference program's by a relative error of at most 0.0095.
Values may be sent and summed in bfloat16 or wider, within the bound.
A program may use at most 128 MiB of HBM per device.

```python
import jax
import jax.numpy as jnp
from jax import lax

CH = 227
LAT = 512
EF = 4
G_DEV = 1024
M_DEV = 512
LINKS_DEV = 2048
GRID = 131072
NODES = 65536
G2M_DEV = 1536
MESH_DEV = 2048
G2M_EDGES = 196608
MESH_EDGES = 262144
SLOT = 16
HG = 256
HM = 128
DEVICES = 128


def banded(key, count, per_block, block_width, reach, limit):
    index = jnp.arange(count, dtype=jnp.int32)
    owner = index // per_block
    lower = jnp.maximum(owner * block_width - reach, 0)
    upper = jnp.minimum((owner + 1) * block_width + reach, limit)
    return jax.random.randint(key, (count,), lower, upper, dtype=jnp.int32)


def draw_g2m_send(key, part):
    return banded(jax.random.fold_in(key, 11), G2M_EDGES, G2M_DEV, G_DEV, HG, GRID)


def draw_g2m_recv(key, part):
    return banded(jax.random.fold_in(key, 12), G2M_EDGES, G2M_DEV, M_DEV, 0, NODES)


def draw_mesh_recv(key, part):
    return banded(jax.random.fold_in(key, 13), MESH_EDGES, MESH_DEV, M_DEV, 0, NODES)


def draw_m2g_send(key, part):
    return banded(jax.random.fold_in(key, 14), 3 * GRID, 3 * G_DEV, M_DEV, HM, NODES)


def place_ends(entries, rng, smallest, high):
    longest = entries.shape.index(max(entries.shape))
    spots = []
    for shift in (0, 1):
        where = [jax.random.randint(jax.random.fold_in(rng, axis), (), 0, length) for axis, length in enumerate(entries.shape)]
        where[longest] = (where[longest] + shift) % entries.shape[longest]
        spots.append(tuple(where))
    return entries.at[spots[0]].set(smallest).at[spots[1]].set(high)


def levels(key, extent, cuts, low, top_value):
    def one(axis_at, shards_of):
        heights = jax.random.uniform(jax.random.fold_in(jax.random.fold_in(key, 6), axis_at), (shards_of,), jnp.float32, low / len(cuts), top_value / len(cuts))
        return jnp.repeat(jnp.exp(heights), extent[axis_at] // shards_of).reshape((-1,) + (1,) * (len(extent) - axis_at - 1))

    gain = one(*cuts[0])
    for cut in cuts[1:]:
        gain = gain * one(*cut)
    return gain


def noise(stream_key, shape, width, bound, shards=(), held_as=jnp.bfloat16):
    level = levels(stream_key, shape, shards, -0.22, 0.18) if shards else 1.0
    values = jax.random.normal(stream_key, shape, jnp.float32) * width * level
    return jnp.minimum(jnp.maximum(values, -bound), bound).astype(held_as)


def setup_inputs(seed: int = 0) -> dict:
    key_of = jax.random.split(jax.random.key(seed), 20)
    grid_in = noise(key_of[0], (CH, GRID), 1.0, 6.0, ((1, 128),))
    grid_embed_w = noise(key_of[1], (LAT, CH), CH ** -0.5, 0.375)
    g2m_w = noise(key_of[2], (LAT, LAT), LAT ** -0.5, 0.25)
    pair_w = noise(key_of[3], (4, 2, LAT, LAT), LAT ** -0.5, 0.25)
    second_w = noise(key_of[4], (5, LAT, LAT), LAT ** -0.5, 0.25)
    first_b = noise(key_of[5], (6, LAT), 1.0, 4.0, (), jnp.float32)
    norm_gain = jnp.clip(jax.random.uniform(key_of[6], (5, LAT), jnp.float32, 0.5, 1.5), 0.5, 1.5)
    geom_w = noise(key_of[7], (3, LAT, EF), EF ** -0.5, 3.0)
    out_w = noise(key_of[8], (CH, LAT), LAT ** -0.5, 0.25)
    out_b = noise(key_of[9], (CH,), 1.0, 4.0, (), jnp.float32)
    g2m_geom = noise(key_of[10], (EF, G2M_EDGES), 1.0, 6.0, ((1, 128),))
    mesh_geom = noise(key_of[11], (EF, MESH_EDGES), 1.0, 6.0, ((1, 128),))
    m2g_geom = noise(key_of[12], (EF, 3 * GRID), 1.0, 6.0, ((1, 128),))
    g2m_send = draw_g2m_send(jax.random.fold_in(key_of[19], 71), 0)
    g2m_recv = draw_g2m_recv(jax.random.fold_in(key_of[19], 71), 0)
    mesh_recv = draw_mesh_recv(jax.random.fold_in(key_of[19], 71), 0)
    mesh_slot = place_ends(jax.random.randint(key_of[16], (MESH_EDGES,), 0, LINKS_DEV), jax.random.fold_in(key_of[16], 1), 0, LINKS_DEV - 1).astype(jnp.int32)
    mesh_rows = place_ends(jax.random.randint(key_of[17], (DEVICES * DEVICES, SLOT), 0, M_DEV), jax.random.fold_in(key_of[17], 1), 0, M_DEV - 1).astype(jnp.int32)
    m2g_send = draw_m2g_send(jax.random.fold_in(key_of[19], 71), 0)
    return dict(grid_in=grid_in, grid_embed_w=grid_embed_w, g2m_w=g2m_w, pair_w=pair_w, second_w=second_w, first_b=first_b, norm_gain=norm_gain, geom_w=geom_w, out_w=out_w, out_b=out_b, g2m_geom=g2m_geom, mesh_geom=mesh_geom, m2g_geom=m2g_geom, g2m_send=g2m_send, g2m_recv=g2m_recv, mesh_recv=mesh_recv, mesh_slot=mesh_slot, mesh_rows=mesh_rows, m2g_send=m2g_send)


eps = 1e-05

def project(weight, values):
    return jnp.dot(weight, values, preferred_element_type=jnp.float32)

def layer_norm(values, gain_rows):
    row_mean = lax.optimization_barrier(jnp.mean(values, axis=0))
    row_var = lax.optimization_barrier(jnp.mean(values * values, axis=0)) - row_mean * row_mean
    return (values - row_mean[None]) * lax.rsqrt(row_var + eps)[None] * gain_rows[:, None]

def node_sums(message, receivers, count):
    return jax.ops.segment_sum(message.astype(jnp.float32).T, receivers, num_segments=count).T

def edge_block(pre_act, weight, gain_rows):
    hidden = jax.nn.silu(pre_act).astype(jnp.bfloat16)
    return layer_norm(project(weight, hidden), gain_rows).astype(jnp.bfloat16)

def reference(grid_in, grid_embed_w, g2m_w, pair_w, second_w, first_b, norm_gain, geom_w, out_w, out_b, g2m_geom, mesh_geom, m2g_geom, g2m_send, g2m_recv, mesh_recv, mesh_slot, mesh_rows, m2g_send):
    grid_latent = edge_block(project(grid_embed_w, grid_in) + first_b[0][:, None], second_w[0], norm_gain[0])
    encode_send = project(g2m_w, grid_latent).astype(jnp.bfloat16)
    pre_act = encode_send[:, g2m_send].astype(jnp.float32) + project(geom_w[0], g2m_geom) + first_b[1][:, None]
    message = edge_block(pre_act, second_w[1], norm_gain[1])
    mesh_latent = node_sums(message, g2m_recv, NODES).astype(jnp.bfloat16)
    link_send = project(pair_w[0, 0], mesh_latent).astype(jnp.bfloat16)
    link_recv = project(pair_w[0, 1], mesh_latent)
    edge_index = jnp.arange(MESH_EDGES, dtype=jnp.int32)
    owner = (edge_index // MESH_DEV).astype(jnp.int32)
    source = (mesh_slot // SLOT).astype(jnp.int32)
    position = (mesh_slot % SLOT).astype(jnp.int32)
    senders = source * M_DEV + mesh_rows[source * DEVICES + owner, position]
    pre_act = link_send[:, senders].astype(jnp.float32) + link_recv[:, mesh_recv] + project(geom_w[1], mesh_geom) + first_b[2][:, None]
    message = edge_block(pre_act, second_w[2], norm_gain[2])
    aggregate = node_sums(message, mesh_recv, NODES).astype(jnp.bfloat16)
    node_pre = project(pair_w[1, 0], mesh_latent) + project(pair_w[1, 1], aggregate) + first_b[3][:, None]
    node_hidden = jax.nn.silu(node_pre).astype(jnp.bfloat16)
    mesh_state = (mesh_latent.astype(jnp.float32) + layer_norm(project(second_w[3], node_hidden), norm_gain[3])).astype(jnp.bfloat16)
    decode_send = project(pair_w[2, 0], mesh_state).astype(jnp.bfloat16)
    decode_grid = project(pair_w[2, 1], grid_latent)
    expanded = jnp.broadcast_to(decode_grid[:, :, None], (LAT, GRID, 3)).reshape(LAT, 3 * GRID)
    pre_act = decode_send[:, m2g_send].astype(jnp.float32) + expanded + project(geom_w[2], m2g_geom) + first_b[4][:, None]
    message = edge_block(pre_act, second_w[4], norm_gain[4])
    gathered = message.astype(jnp.float32).reshape(LAT, GRID, 3).sum(axis=2).astype(jnp.bfloat16)
    out_pre = project(pair_w[3, 0], grid_latent) + project(pair_w[3, 1], gathered) + first_b[5][:, None]
    out_hidden = jax.nn.silu(out_pre).astype(jnp.bfloat16)
    prediction = project(out_w, out_hidden) + out_b[:, None]
    return (prediction, mesh_state)
```

```python
import functools

import jax
import jax.numpy as jnp
from jax import lax
from jax.experimental import pallas as pl
from jax.experimental.pallas import tpu as pltpu
from jax.sharding import PartitionSpec as P

EPS = 1e-05
BF = jnp.bfloat16
F32 = jnp.float32
AXES = ("space", "chan")


def dot(a, b):
    return lax.dot_general(a, b, (((1,), (0,)), ((), ())), preferred_element_type=F32)


def dot_nt(a, b):
    return lax.dot_general(a, b, (((1,), (1,)), ((), ())), preferred_element_type=F32)


def dot_tn(a, b):
    return lax.dot_general(a, b, (((0,), (0,)), ((), ())), preferred_element_type=F32)


def silu(v):
    u = 0.5 * v
    return u + u * jnp.tanh(u)


def normed(y):
    n = y.shape[0]
    m = jnp.sum(y, axis=0, keepdims=True) * (1.0 / n)
    s = jnp.sum(y * y, axis=0, keepdims=True) * (1.0 / n)
    r = lax.rsqrt(s - m * m + EPS)
    return y * r - m * r


def one_hot(row, n):
    lanes = row.shape[1]
    return (lax.broadcasted_iota(jnp.int32, (n, lanes), 0) == row).astype(BF)


def columns_of(rows_ref, fb_ref, ng_ref, ob_ref=None):
    rows_ref[...] = jnp.zeros_like(rows_ref)
    rows_ref[0:6, :] = fb_ref[...]
    rows_ref[8:13, :] = ng_ref[...]
    if ob_ref is not None:
        rows_ref[16:17, 0 : ob_ref.shape[1]] = ob_ref[...]
    return rows_ref[...].T


def edge_columns(vec_ref, gwt_ref, bias):
    vec_ref[...] = jnp.zeros_like(vec_ref)
    vec_ref[0:4, :] = gwt_ref[0].astype(F32)
    for k in range(3):
        head = bias.astype(BF).astype(F32)
        vec_ref[4 + k : 5 + k, :] = head
        bias = bias - head
    return vec_ref[...].T.astype(BF)


def with_features(hot, feats):
    zeros = jnp.zeros((128 - feats.shape[0], feats.shape[1]), BF)
    return jnp.concatenate([hot, feats, zeros], axis=0)


def encode_kernel(
    cells,
    nodes,
    gin,
    we,
    w2a,
    g2m,
    w2b,
    p00,
    fb,
    ng,
    gw,
    geom,
    send,
    recv,
    rows,
    lat_out,
    ml_out,
    out_rows,
    vec,
    cols,
    sent,
    acc,
    embed,
):
    cols[...] = columns_of(vec, fb, ng)
    ext = gin.shape[1]
    embed[...] = jnp.zeros_like(embed)
    embed[:, 0 : we.shape[1]] = we[...]
    sent[:, ext:] = edge_columns(vec, gw, fb[1:2, :])
    halo = (ext - cells) // 2
    w = 256
    for i in range(ext // w):
        at = slice(i * w, (i + 1) * w)
        h = silu(dot(embed[...], gin[:, at]) + cols[:, 0:1]).astype(BF)
        lat = (normed(dot(w2a[0], h)) * cols[:, 8:9]).astype(BF)
        if halo <= i * w < halo + cells:
            lat_out[:, i * w - halo : (i + 1) * w - halo] = lat
        sent[:, at] = dot(g2m[...], lat).astype(BF)
    edges = send.shape[1]
    acc[...] = jnp.zeros_like(acc)
    for i in range(edges // w):
        at = slice(i * w, (i + 1) * w)
        pre = dot(sent[...], with_features(one_hot(send[:, at], ext), geom[:, at]))
        message = normed(dot(w2b[0], silu(pre).astype(BF))).astype(BF)
        acc[...] += dot_nt(message, one_hot(recv[:, at], nodes))
    ml = (acc[...] * cols[:, 9:10]).astype(BF)
    ml_out[...] = ml
    link = dot_nt(ml.astype(F32).T.astype(BF), p00[0, 0]).astype(BF)
    for i in range(rows.shape[1] // w):
        at = slice(i * w, (i + 1) * w)
        out_rows[at, :] = dot_tn(one_hot(rows[:, at], nodes), link).astype(BF)


def mesh_kernel(
    arrived,
    ml,
    p01,
    w2c,
    p10,
    p11,
    w2d,
    p20,
    fb,
    ng,
    gw,
    geom,
    slot,
    recv,
    state_out,
    ds_out,
    vec,
    cols,
    arr_t,
    acc,
):
    cols[...] = columns_of(vec, fb, ng)
    nodes = ml.shape[1]
    slots = arrived.shape[0]
    w = 256
    for i in range(slots // w):
        at = slice(i * w, (i + 1) * w)
        arr_t[:, at] = arrived[at, :].T
    link = dot(p01[0, 0], ml[...]).astype(BF)
    arr_t[:, slots:] = edge_columns(vec, gw, fb[2:3, :])
    acc[...] = jnp.zeros_like(acc)
    for i in range(slot.shape[1] // w):
        at = slice(i * w, (i + 1) * w)
        to = one_hot(recv[:, at], nodes)
        pre = (
            dot(arr_t[...], with_features(one_hot(slot[:, at], slots), geom[:, at]))
            + dot(link, to)
        )
        message = normed(dot(w2c[0], silu(pre).astype(BF))).astype(BF)
        acc[...] += dot_nt(message, to)
    aggregate = (acc[...] * cols[:, 10:11]).astype(BF)
    hidden = silu(dot(p10[0, 0], ml[...]) + dot(p11[0, 0], aggregate) + cols[:, 3:4]).astype(BF)
    state = (ml[...].astype(F32) + normed(dot(w2d[0], hidden)) * cols[:, 11:12]).astype(BF)
    state_out[...] = state
    ds_out[...] = dot(p20[0, 0], state).astype(BF)


def decode_kernel(
    ds,
    lat,
    p21,
    p30,
    p31,
    w2e,
    ow,
    fb,
    ng,
    ob,
    gw,
    geom,
    send,
    pred_out,
    vec,
    cols,
    sent,
):
    cols[...] = columns_of(vec, fb, ng, ob)
    cells = lat.shape[1]
    reach = ds.shape[1]
    outs = ow.shape[0]
    sent[:, 0:reach] = ds[...]
    sent[:, reach:] = edge_columns(vec, gw, fb[4:5, :])
    w = 256
    for i in range(cells // w):
        at = slice(i * w, (i + 1) * w)
        here = lat[:, at]
        base = dot(p21[0, 0], here)
        total = jnp.zeros_like(base)
        for j in range(3):
            hot = one_hot(send[j : j + 1, at], reach)
            pre = base + dot(sent[...], with_features(hot, geom[16 * j : 16 * j + 16, at]))
            message = normed(dot(w2e[0], silu(pre).astype(BF))).astype(BF)
            total += message.astype(F32)
        gathered = (total * cols[:, 12:13]).astype(BF)
        pre = dot(p30[0, 0], here) + dot(p31[0, 0], gathered) + cols[:, 5:6]
        pred_out[:, at] = dot(ow[...], silu(pre).astype(BF)) + cols[0:outs, 16:17]


def whole(x):
    nd = x.ndim
    return pl.BlockSpec(x.shape, lambda i: (0,) * nd)


def part(x, *index):
    nd = x.ndim
    lead = len(index)
    block = (1,) * lead + x.shape[lead:]
    full = tuple(index) + (0,) * (nd - lead)
    return pl.BlockSpec(block, lambda i: full)


def call(kernel, args, specs, outs, scratch, name):
    return pl.pallas_call(
        kernel,
        grid=(1,),
        in_specs=specs,
        out_specs=[whole(o) for o in outs],
        out_shape=outs,
        scratch_shapes=scratch,
        compiler_params=pltpu.CompilerParams(vmem_limit_bytes=56 << 20),
        name=name,
    )(*args)


def ends(x, width):
    n = lax.axis_size(AXES)
    forward = [(i, i + 1) for i in range(n - 1)]
    backward = [(b, a) for a, b in forward]
    low = lax.ppermute(x[:, x.shape[1] - width :], AXES, forward)
    high = lax.ppermute(x[:, :width], AXES, backward)
    return jnp.concatenate([low, x, high], axis=1)


def features(geom):
    return jnp.concatenate([geom, jnp.ones((3, geom.shape[1]), BF), jnp.zeros((9, geom.shape[1]), BF)])


def body(
    grid_in,
    grid_embed_w,
    g2m_w,
    pair_w,
    second_w,
    first_b,
    norm_gain,
    geom_w,
    out_w,
    out_b,
    g2m_geom,
    mesh_geom,
    m2g_geom,
    g2m_send,
    g2m_recv,
    mesh_recv,
    mesh_slot,
    mesh_rows,
    m2g_send,
):
    width = grid_embed_w.shape[0]
    cells = grid_in.shape[1]
    devices = mesh_rows.shape[0]
    nodes = 512
    position = lax.axis_index(AXES)
    shape = jax.ShapeDtypeStruct
    vec = pltpu.VMEM((128, width), F32)
    cols = pltpu.VMEM((width, 128), F32)

    reach = cells // 4
    gin = jnp.pad(ends(grid_in, reach), ((0, 256 - grid_in.shape[0]), (0, 0)))
    geom_wt = geom_w.transpose(0, 2, 1)
    send = (g2m_send - position * cells + reach).reshape(1, -1)
    recv = (g2m_recv - position * nodes).reshape(1, -1)
    rows = mesh_rows.reshape(1, -1)
    args = (gin, grid_embed_w, second_w, g2m_w, second_w, pair_w, first_b, norm_gain, geom_wt)
    geom = features(g2m_geom)
    args += (geom, send, recv, rows)
    specs = [
        whole(gin),
        whole(grid_embed_w),
        part(second_w, 0),
        whole(g2m_w),
        part(second_w, 1),
        part(pair_w, 0, 0),
        whole(first_b),
        whole(norm_gain),
        part(geom_wt, 0),
        whole(geom),
        whole(send),
        whole(recv),
        whole(rows),
    ]
    lat, ml, outgoing = call(
        functools.partial(encode_kernel, cells, nodes),
        args,
        specs,
        [shape((width, cells), BF), shape((width, nodes), BF), shape((rows.shape[1], width), BF)],
        [
            vec,
            cols,
            pltpu.VMEM((width, gin.shape[1] + 128), BF),
            pltpu.VMEM((width, nodes), F32),
            pltpu.VMEM((width, 256), BF),
        ],
        "encode",
    )

    arrived = lax.all_to_all(
        outgoing.reshape(devices, -1, width), AXES, split_axis=0, concat_axis=0, tiled=True
    ).reshape(-1, width)

    slot = mesh_slot.reshape(1, -1)
    recv = (mesh_recv - position * nodes).reshape(1, -1)
    args = (arrived, ml, pair_w, second_w, pair_w, pair_w, second_w, pair_w, first_b, norm_gain, geom_wt)
    geom = features(mesh_geom)
    args += (geom, slot, recv)
    specs = [
        whole(arrived),
        whole(ml),
        part(pair_w, 0, 1),
        part(second_w, 2),
        part(pair_w, 1, 0),
        part(pair_w, 1, 1),
        part(second_w, 3),
        part(pair_w, 2, 0),
        whole(first_b),
        whole(norm_gain),
        part(geom_wt, 1),
        whole(geom),
        whole(slot),
        whole(recv),
    ]
    state, ds = call(
        mesh_kernel,
        args,
        specs,
        [shape((width, nodes), BF), shape((width, nodes), BF)],
        [vec, cols, pltpu.VMEM((width, arrived.shape[0] + 128), BF), pltpu.VMEM((width, nodes), F32)],
        "mesh",
    )

    reach = nodes // 4
    ds = ends(ds, reach)
    send = (m2g_send - position * nodes + reach).reshape(cells, 3).T
    geom = features(m2g_geom).reshape(16, cells, 3).transpose(2, 0, 1).reshape(48, cells)
    ob = out_b.reshape(1, -1)
    args = (ds, lat, pair_w, pair_w, pair_w, second_w, out_w, first_b, norm_gain, ob, geom_wt, geom, send)
    specs = [
        whole(ds),
        whole(lat),
        part(pair_w, 2, 1),
        part(pair_w, 3, 0),
        part(pair_w, 3, 1),
        part(second_w, 4),
        whole(out_w),
        whole(first_b),
        whole(norm_gain),
        whole(ob),
        part(geom_wt, 2),
        whole(geom),
        whole(send),
    ]
    (prediction,) = call(
        decode_kernel,
        args,
        specs,
        [shape((out_w.shape[0], cells), F32)],
        [vec, cols, pltpu.VMEM((width, ds.shape[1] + 128), BF)],
        "decode",
    )
    return (prediction, state)


def solution(mesh):
    return jax.shard_map(
        body,
        mesh=mesh,
        in_specs=(
            P(None, AXES),
            P(),
            P(),
            P(),
            P(),
            P(),
            P(),
            P(),
            P(),
            P(),
            P(None, AXES),
            P(None, AXES),
            P(None, AXES),
            P(AXES),
            P(AXES),
            P(AXES),
            P(AXES),
            P(AXES, None),
            P(AXES),
        ),
        out_specs=(P(None, AXES), P(None, AXES)),
        check_vma=False,
    )
```

```python
import functools

import jax
import jax.numpy as jnp
from jax import lax
from jax.experimental import pallas as pl
from jax.experimental.pallas import tpu as pltpu
from jax.sharding import PartitionSpec as P

EPS = 1e-05
BF = jnp.bfloat16
F32 = jnp.float32
AXES = ("space", "chan")
MESH = pl.DeviceIdType.MESH


def dot(a, b):
    return lax.dot_general(a, b, (((1,), (0,)), ((), ())), preferred_element_type=F32)


def dot_nt(a, b):
    return lax.dot_general(a, b, (((1,), (1,)), ((), ())), preferred_element_type=F32)


def dot_tn(a, b):
    return lax.dot_general(a, b, (((0,), (0,)), ((), ())), preferred_element_type=F32)


def silu(v):
    u = 0.5 * v
    return u + u * jnp.tanh(u)


def normed(y):
    n = y.shape[0]
    m = jnp.sum(y, axis=0, keepdims=True) * (1.0 / n)
    s = jnp.sum(y * y, axis=0, keepdims=True) * (1.0 / n)
    r = lax.rsqrt(s - m * m + EPS)
    return y * r - m * r


def one_hot(row, n):
    return (lax.broadcasted_iota(jnp.int32, (n, row.shape[1]), 0) == row).astype(BF)


def edge_columns(vec, gwt, bias):
    vec[...] = jnp.zeros_like(vec)
    vec[0:4, :] = gwt.astype(F32)
    for k in range(3):
        head = bias.astype(BF).astype(F32)
        vec[4 + k : 5 + k, :] = head
        bias = bias - head
    return vec[...].T.astype(BF)


def with_features(hot, feats):
    zeros = jnp.zeros((128 - feats.shape[0], feats.shape[1]), BF)
    return jnp.concatenate([hot, feats, zeros], axis=0)


def fill_features(ref, geom):
    ref[...] = jnp.zeros_like(ref)
    ref[0:4, :] = geom[...].astype(F32)
    ref[4:7, :] = jnp.ones((3, ref.shape[1]), F32)


def kernel(
    gin,
    wet,
    g2m,
    pair,
    second,
    fb,
    ng,
    gwt,
    ow,
    ob,
    geom1,
    geom2,
    geom3,
    send1,
    recv1,
    recv2,
    slot,
    rows_t,
    send3,
    pred_out,
    state_out,
    w_e,
    w_g,
    w_p,
    w_s,
    w_o,
    own,
    low,
    high,
    ginx,
    embed,
    vec,
    cols,
    feat1,
    feat2,
    feat3,
    feat4,
    sent,
    lat,
    base,
    outp,
    acc,
    ml,
    rows,
    outgoing,
    arrived,
    pre,
    ds,
    send4,
    w_sem,
    halo_send,
    halo_recv,
    a2a_send,
    a2a_recv,
    stage,
):
    s, c = lax.axis_index("space"), lax.axis_index("chan")
    me = s * 16 + c
    x, core, z, y = s // 2, s % 2, c // 4, c % 4
    cells, nodes = own.shape[1], ml.shape[1]
    reach1 = low.shape[1]
    reach3 = nodes // 4
    ext = cells + 2 * reach1
    width = ml.shape[0]

    def flat(d):
        d = (d + 128) % 128
        return (d // 16, d % 16)

    left, right = flat(me - 1), flat(me + 1)
    y_peers = [(s, z * 4 + (y + k) % 4) for k in (1, 2, 3)]
    z_peers = [(s, (z + k) % 4 * 4 + y) for k in (1, 2, 3)]
    x_peers = [((x + k) % 4 * 2 + core, c) for k in (1, 2, 3)]
    partners = [left, right, (x * 2 + 1 - core, c)] + y_peers + z_peers + x_peers
    barrier = pltpu.get_barrier_semaphore()
    for peer in partners:
        pl.semaphore_signal(barrier, inc=1, device_id=peer, device_id_type=MESH)

    def meet(k, peers):
        for peer in peers:
            pl.semaphore_signal(stage.at[k], inc=1, device_id=peer, device_id_type=MESH)

    copies = {}

    def fetch(name, src, dst):
        copies[name] = pltpu.make_async_copy(src, dst, w_sem.at[len(copies)])
        copies[name].start()

    fetch("own", gin, own)
    fetch("we", wet, w_e)
    fetch("s0", second.at[0], w_s.at[0])
    fetch("g2m", g2m, w_g)
    fetch("s1", second.at[1], w_s.at[1])
    fetch("p00", pair.at[0, 0], w_p.at[0, 0])
    fetch("p21", pair.at[2, 1], w_p.at[2, 1])
    fetch("p30", pair.at[3, 0], w_p.at[3, 0])
    fetch("p01", pair.at[0, 1], w_p.at[0, 1])
    fetch("s2", second.at[2], w_s.at[2])
    fetch("p10", pair.at[1, 0], w_p.at[1, 0])
    fetch("p11", pair.at[1, 1], w_p.at[1, 1])
    fetch("s3", second.at[3], w_s.at[3])
    fetch("p20", pair.at[2, 0], w_p.at[2, 0])
    fetch("s4", second.at[4], w_s.at[4])
    fetch("p31", pair.at[3, 1], w_p.at[3, 1])
    fetch("ow", ow, w_o)

    vec[...] = jnp.zeros_like(vec)
    vec[0:6, :] = fb[...]
    vec[8:13, :] = ng[...]
    vec[16:17, 0 : ob.shape[1]] = ob[...]
    cols[...] = vec[...].T
    embed[...] = jnp.zeros_like(embed)
    ginx[...] = jnp.zeros_like(ginx)
    sent[:, ext:] = edge_columns(vec, gwt[0], fb[1:2, :])
    fill_features(feat1, geom1)

    copies["own"].wait()
    copies["we"].wait()
    channels = own.shape[0]
    embed[0:channels, :] = w_e[...]

    pl.semaphore_wait(barrier, len(partners))
    to_right = pltpu.make_async_remote_copy(
        own.at[:, cells - reach1 :], low, halo_send.at[0], halo_recv.at[0], device_id=right, device_id_type=MESH
    )
    to_left = pltpu.make_async_remote_copy(
        own.at[:, 0:reach1], high, halo_send.at[1], halo_recv.at[1], device_id=left, device_id_type=MESH
    )
    to_right.start()
    to_left.start()
    meet(0, y_peers)

    def embedded(values):
        h = silu(dot_tn(embed[...], values) + cols[:, 0:1]).astype(BF)
        return (normed(dot(w_s[0], h)) * cols[:, 8:9]).astype(BF)

    ginx[0:channels, reach1 : reach1 + cells] = own[...]
    copies["s0"].wait()
    copies["g2m"].wait()
    lat[...] = embedded(ginx[:, reach1 : reach1 + cells])
    sent[:, reach1 : reach1 + cells] = dot(w_g[...], lat[...]).astype(BF)
    pl.semaphore_wait(stage.at[0], 3)
    meet(1, z_peers)

    spread = (
        lax.broadcasted_iota(jnp.int32, (128, rows.shape[1]), 0)
        == lax.broadcasted_iota(jnp.int32, (128, rows.shape[1]), 1) // 16
    ).astype(BF)
    lists = rows_t[...]
    picked = dot((lists // 16).astype(F32).astype(BF), spread) * 16.0 + dot(
        (lists % 16).astype(F32).astype(BF), spread
    )
    mine = (
        lax.broadcasted_iota(jnp.int32, picked.shape, 0)
        == lax.broadcasted_iota(jnp.int32, picked.shape, 1) % 16
    )
    rows[...] = jnp.sum(jnp.where(mine, picked, 0.0), axis=0, keepdims=True).astype(jnp.int32)

    to_right.wait()
    to_left.wait()
    ginx[0:channels, 0:reach1] = low[...]
    ginx[0:channels, reach1 + cells :] = high[...]
    ends = embedded(jnp.concatenate([ginx[:, 0:reach1], ginx[:, reach1 + cells :]], axis=1))
    ends = dot(w_g[...], ends).astype(BF)
    sent[:, 0:reach1] = ends[:, 0:reach1]
    sent[:, reach1 + cells : ext] = ends[:, reach1:]
    pl.semaphore_wait(stage.at[1], 3)
    meet(2, x_peers)

    w = 512
    acc[...] = jnp.zeros_like(acc)
    copies["s1"].wait()
    first1 = me * cells - reach1

    @pl.loop(0, send1.shape[0] // w)
    def _(i):
        at = pl.ds(pl.multiple_of(i * w, w), w)
        hot = one_hot(send1[at].reshape(1, w) - first1, ext)
        v = dot(sent[...], with_features(hot, feat1[:, at].astype(BF)))
        message = normed(dot(w_s[1], silu(v).astype(BF))).astype(BF)
        acc[...] += dot_nt(message, one_hot(recv1[at].reshape(1, w) - me * nodes, nodes))

    ml[...] = (acc[...] * cols[:, 9:10]).astype(BF)
    copies["p00"].wait()
    link = dot_nt(ml[...].astype(F32).T.astype(BF), w_p[0, 0]).astype(BF)
    pl.semaphore_wait(stage.at[2], 3)

    def out_copy(i, k):
        to_s, to_c = (s + i) % 8, (c + k) % 16
        to = to_s * 16 + to_c
        return pltpu.make_async_remote_copy(
            outgoing.at[pl.ds(to * 16, 16)],
            arrived.at[pl.ds(me * 16, 16)],
            a2a_send,
            a2a_recv.at[i],
            device_id=(to_s, to_c),
            device_id_type=MESH,
        )

    def make_rows(i):
        at = pl.ds(pl.multiple_of((s + i) % 8 * 256, 256), 256)
        outgoing[at, :] = dot_tn(one_hot(rows[:, at], nodes), link).astype(BF)

    @pl.loop(1, 8)
    def _(i):
        make_rows(i)

        @pl.loop(0, 16)
        def _(k):
            out_copy(i, k).start()

    make_rows(0)

    @pl.loop(1, 16)
    def _(k):
        out_copy(0, k).start()

    here = pl.ds(pl.multiple_of(me * 16, 16), 16)
    arrived[here, :] = outgoing[here, :]

    fill_features(feat2, geom2)
    fill_features(feat3, geom3)
    edges = pl.ds(0, w)
    copies["p01"].wait()
    own_link = jnp.concatenate(
        [dot(w_p[0, 1], ml[...]).astype(BF), edge_columns(vec, gwt[1], fb[2:3, :])], axis=1
    )

    @pl.loop(0, slot.shape[0] // w)
    def _(i):
        at = pl.ds(pl.multiple_of(i * w, w), w)
        hot = one_hot(recv2[at].reshape(1, w) - me * nodes, nodes)
        pre[:, at] = dot(own_link, with_features(hot, feat2[:, at].astype(BF)))

    copies["p21"].wait()
    copies["p30"].wait()
    base[...] = dot(w_p[2, 1], lat[...])
    outp[...] = dot(w_p[3, 0], lat[...]) + cols[:, 5:6]

    local = send3[...].reshape(1, 3 * cells) - (me * nodes - reach3)
    feat3[8:9, :] = (local // 16).astype(F32)
    feat3[9:10, :] = (local % 16).astype(F32)
    ds[:, nodes + 2 * reach3 :] = edge_columns(vec, gwt[2], fb[4:5, :])

    for q in range(cells // 256):
        part = feat3[:, q * 768 : (q + 1) * 768].astype(BF)
        for j in range(3):
            take = (
                lax.broadcasted_iota(jnp.int32, (768, 256), 0)
                == 3 * lax.broadcasted_iota(jnp.int32, (768, 256), 1) + j
            ).astype(BF)
            got = dot(part, take)
            at = (3 * (q // 2) + j) * w + q % 2 * 256
            feat4[:, at : at + 256] = got
            send4[:, at : at + 256] = (got[8:9, :] * 16.0 + got[9:10, :]).astype(jnp.int32)
    feat4[8:16, :] = jnp.zeros((8, feat4.shape[1]), F32)

    def take_rows(i, count):
        got = arrived.at[pl.ds(0, 16 * count)]
        pltpu.make_async_copy(got, got, a2a_recv.at[i]).wait()
        start = pl.multiple_of((s + 8 - i) % 8 * 256, 256)
        block = arrived[pl.ds(start, 256), :]

        @pl.loop(0, slot.shape[0] // w)
        def _(e):
            at = pl.ds(pl.multiple_of(e * w, w), w)
            pre[:, at] += dot_tn(block, one_hot(slot[at].reshape(1, w) - start, 256))

    @pl.loop(1, 8)
    def _(i):
        take_rows(i, 16)

    take_rows(0, 15)
    gone = outgoing.at[pl.ds(0, 16 * 127)]
    pltpu.make_async_copy(gone, gone, a2a_send).wait()

    acc[...] = jnp.zeros_like(acc)
    copies["s2"].wait()

    @pl.loop(0, slot.shape[0] // w)
    def _(i):
        at = pl.ds(pl.multiple_of(i * w, w), w)
        message = normed(dot(w_s[2], silu(pre[:, at]).astype(BF))).astype(BF)
        acc[...] += dot_nt(message, one_hot(recv2[at].reshape(1, w) - me * nodes, nodes))

    for name in ("p10", "p11", "s3", "p20"):
        copies[name].wait()

    def update(latent, total):
        aggregate = (total * cols[:, 10:11]).astype(BF)
        hidden = silu(dot(w_p[1, 0], latent) + dot(w_p[1, 1], aggregate) + cols[:, 3:4]).astype(BF)
        state = (latent.astype(F32) + normed(dot(w_s[3], hidden)) * cols[:, 11:12]).astype(BF)
        return state, dot(w_p[2, 0], state).astype(BF)

    last = nodes - reach3
    both = lambda ref: jnp.concatenate([ref[:, 0:reach3], ref[:, last:]], axis=1)
    state, out = update(both(ml), both(acc))
    state_out[:, 0:reach3] = state[:, 0:reach3]
    state_out[:, last:] = state[:, reach3:]
    ds[:, reach3 : 2 * reach3] = out[:, 0:reach3]
    ds[:, nodes : nodes + reach3] = out[:, reach3:]
    to_right = pltpu.make_async_remote_copy(
        ds.at[:, nodes : nodes + reach3],
        ds.at[:, 0:reach3],
        halo_send.at[2],
        halo_recv.at[2],
        device_id=right,
        device_id_type=MESH,
    )
    to_left = pltpu.make_async_remote_copy(
        ds.at[:, reach3 : 2 * reach3],
        ds.at[:, nodes + reach3 : nodes + 2 * reach3],
        halo_send.at[3],
        halo_recv.at[3],
        device_id=left,
        device_id_type=MESH,
    )
    to_right.start()
    to_left.start()
    state, out = update(ml[:, reach3:last], acc[:, reach3:last])
    state_out[:, reach3:last] = state
    ds[:, 2 * reach3 : nodes] = out
    for name in ("s4", "p31", "ow"):
        copies[name].wait()
    to_right.wait()
    to_left.wait()

    outs = ow.shape[0]

    @pl.loop(0, cells // w)
    def _(q):
        at = pl.ds(pl.multiple_of(q * w, w), w)
        total = jnp.zeros((width, w), F32)
        for j in range(3):
            edge = pl.ds(pl.multiple_of((3 * q + j) * w, w), w)
            hot = one_hot(send4[:, edge], nodes + 2 * reach3)
            v = base[:, at] + dot(ds[...], with_features(hot, feat4[:, edge].astype(BF)))
            total += normed(dot(w_s[4], silu(v).astype(BF))).astype(BF).astype(F32)
        gathered = (total * cols[:, 12:13]).astype(BF)
        hidden = silu(outp[:, at] + dot(w_p[3, 1], gathered)).astype(BF)
        pred_out[:, at] = dot(w_o[...], hidden) + cols[0:outs, 16:17]


def body(
    grid_in,
    grid_embed_w,
    g2m_w,
    pair_w,
    second_w,
    first_b,
    norm_gain,
    geom_w,
    out_w,
    out_b,
    g2m_geom,
    mesh_geom,
    m2g_geom,
    g2m_send,
    g2m_recv,
    mesh_recv,
    mesh_slot,
    mesh_rows,
    m2g_send,
):
    width, channels = grid_embed_w.shape
    cells = grid_in.shape[1]
    nodes = 512
    links = mesh_rows.size
    reach = cells // 4
    ext = cells + 2 * reach
    outs = out_w.shape[0]
    args = (
        grid_in,
        grid_embed_w.T,
        g2m_w,
        pair_w,
        second_w,
        first_b,
        norm_gain,
        geom_w.transpose(0, 2, 1),
        out_w,
        out_b.reshape(1, -1),
        g2m_geom,
        mesh_geom,
        m2g_geom,
        g2m_send,
        g2m_recv,
        mesh_recv,
        mesh_slot,
        mesh_rows.T,
        m2g_send,
    )
    hbm, vmem = pl.BlockSpec(memory_space=pl.ANY), pl.BlockSpec(memory_space=pltpu.VMEM)
    in_specs = [vmem] * len(args)
    for k in (0, 1, 2, 3, 4, 8):
        in_specs[k] = hbm
    V = pltpu.VMEM
    return tuple(
        pl.pallas_call(
            kernel,
            in_specs=in_specs,
            out_specs=[vmem, vmem],
            out_shape=[
                jax.ShapeDtypeStruct((outs, cells), F32),
                jax.ShapeDtypeStruct((width, nodes), BF),
            ],
            scratch_shapes=[
                V((channels, width), BF),
                V((width, width), BF),
                V(pair_w.shape, BF),
                V(second_w.shape, BF),
                V(out_w.shape, BF),
                V((channels, cells), BF),
                V((channels, reach), BF),
                V((channels, reach), BF),
                V((256, ext), BF),
                V((256, width), BF),
                V((128, width), F32),
                V((width, 128), F32),
                V((16, g2m_send.shape[0]), F32),
                V((16, mesh_slot.shape[0]), F32),
                V((16, m2g_send.shape[0]), F32),
                V((16, m2g_send.shape[0]), F32),
                V((width, ext + 128), BF),
                V((width, cells), BF),
                V((width, cells), F32),
                V((width, cells), F32),
                V((width, nodes), F32),
                V((width, nodes), BF),
                V((1, links), jnp.int32),
                V((links, width), BF),
                V((links, width), BF),
                V((width, mesh_slot.shape[0]), F32),
                V((width, nodes + nodes // 2 + 128), BF),
                V((1, m2g_send.shape[0]), jnp.int32),
                pltpu.SemaphoreType.DMA((17,)),
                pltpu.SemaphoreType.DMA((4,)),
                pltpu.SemaphoreType.DMA((4,)),
                pltpu.SemaphoreType.DMA,
                pltpu.SemaphoreType.DMA((8,)),
                pltpu.SemaphoreType.REGULAR((3,)),
            ],
            compiler_params=pltpu.CompilerParams(
                collective_id=0, has_side_effects=True, vmem_limit_bytes=60 << 20
            ),
            name="graph",
        )(*args)
    )


def solution(mesh):
    return jax.shard_map(
        body,
        mesh=mesh,
        in_specs=(
            P(None, AXES),
            P(),
            P(),
            P(),
            P(),
            P(),
            P(),
            P(),
            P(),
            P(),
            P(None, AXES),
            P(None, AXES),
            P(None, AXES),
            P(AXES),
            P(AXES),
            P(AXES),
            P(AXES),
            P(AXES, None),
            P(AXES),
        ),
        out_specs=(P(None, AXES), P(None, AXES)),
        check_vma=False,
    )
```

```python
import functools

import jax
import jax.numpy as jnp
from jax import lax
from jax.experimental import pallas as pl
from jax.experimental.pallas import tpu as pltpu
from jax.sharding import PartitionSpec as P

EPS = 1e-05
BF = jnp.bfloat16
F32 = jnp.float32
AXES = ("space", "chan")
MESH = pl.DeviceIdType.MESH


def dot(a, b):
    return lax.dot_general(a, b, (((1,), (0,)), ((), ())), preferred_element_type=F32)


def dot_nt(a, b):
    return lax.dot_general(a, b, (((1,), (1,)), ((), ())), preferred_element_type=F32)


def dot_tn(a, b):
    return lax.dot_general(a, b, (((0,), (0,)), ((), ())), preferred_element_type=F32)


def silu(v):
    u = 0.5 * v
    return u + u * jnp.tanh(u)


def normed(y):
    n = y.shape[0]
    m = jnp.sum(y, axis=0, keepdims=True) * (1.0 / n)
    s = jnp.sum(y * y, axis=0, keepdims=True) * (1.0 / n)
    r = lax.rsqrt(s - m * m + EPS)
    return y * r - m * r


def one_hot(row, n):
    return (lax.broadcasted_iota(jnp.int32, (n, row.shape[1]), 0) == row).astype(BF)


def edge_columns(vec, gwt, bias):
    vec[...] = jnp.zeros_like(vec)
    vec[0:4, :] = gwt.astype(F32)
    for k in range(3):
        head = bias.astype(BF).astype(F32)
        vec[4 + k : 5 + k, :] = head
        bias = bias - head
    return vec[...].T.astype(BF)


def features(geom, extra=()):
    n = geom.shape[1]
    rows = [geom.astype(F32), jnp.ones((3, n), F32), jnp.zeros((1, n), F32)]
    return jnp.concatenate(rows + list(extra) + [jnp.zeros((8 - len(extra), n), F32)], axis=0)


def padded(feats):
    return jnp.concatenate([feats, jnp.zeros((256 - feats.shape[0], feats.shape[1]), F32)], axis=0).astype(BF)


def kernel(
    gin,
    wet,
    g2m,
    pair,
    second,
    fb,
    ng,
    gwt,
    ow,
    ob,
    geom1,
    geom2,
    geom3,
    send1,
    recv1,
    recv2,
    slot,
    rows_t,
    send3,
    pred_hbm,
    state_hbm,
    w_e,
    w_g,
    w_p,
    w_s,
    w_o,
    own,
    low,
    high,
    ginx,
    embed,
    vec,
    cols,
    feat,
    sent,
    lat,
    outp,
    acc,
    ml,
    outgoing,
    arrived,
    pre,
    pre3,
    ds,
    send4,
    pred_out,
    state_out,
    w_sem,
    halo_send,
    halo_recv,
    a2a_send,
    a2a_recv,
    out_sem,
    stage,
):
    s, c = lax.axis_index("space"), lax.axis_index("chan")
    me = s * 16 + c
    x, core, z, y = s // 2, s % 2, c // 4, c % 4
    cells, nodes = own.shape[1], ml.shape[1]
    reach1 = low.shape[1]
    reach3 = nodes // 4
    ext = cells + 2 * reach1
    width, links = ml.shape[0], arrived.shape[0]
    near3 = nodes + 2 * reach3

    def flat(d):
        d = (d + 128) % 128
        return (d // 16, d % 16)

    left, right = flat(me - 1), flat(me + 1)
    y_peers = [(s, z * 4 + (y + k) % 4) for k in (1, 2, 3)]
    z_peers = [(s, (z + k) % 4 * 4 + y) for k in (1, 2, 3)]
    x_peers = [((x + k) % 4 * 2 + core, c) for k in (1, 2, 3)]
    partners = [left, right, (x * 2 + 1 - core, c)] + y_peers + z_peers + x_peers
    barrier = pltpu.get_barrier_semaphore()
    for peer in partners:
        pl.semaphore_signal(barrier, inc=1, device_id=peer, device_id_type=MESH)

    def meet(k, peers):
        for peer in peers:
            pl.semaphore_signal(stage.at[k], inc=1, device_id=peer, device_id_type=MESH)

    copies = {}

    def fetch(name, src, dst):
        copies[name] = pltpu.make_async_copy(src, dst, w_sem.at[len(copies)])
        copies[name].start()

    fetch("own", gin, own)
    fetch("we", wet, w_e)
    fetch("s0", second.at[0], w_s.at[0])
    fetch("g2m", g2m, w_g)
    fetch("s1", second.at[1], w_s.at[1])
    fetch("p00", pair.at[0, 0], w_p.at[0, 0])
    fetch("p01", pair.at[0, 1], w_p.at[0, 1])
    fetch("p21", pair.at[2, 1], w_p.at[2, 1])
    fetch("p30", pair.at[3, 0], w_p.at[3, 0])
    fetch("s2", second.at[2], w_s.at[2])
    fetch("p10", pair.at[1, 0], w_p.at[1, 0])
    fetch("p11", pair.at[1, 1], w_p.at[1, 1])
    fetch("s3", second.at[3], w_s.at[3])
    fetch("p20", pair.at[2, 0], w_p.at[2, 0])
    fetch("s4", second.at[4], w_s.at[4])
    fetch("p31", pair.at[3, 1], w_p.at[3, 1])
    fetch("ow", ow, w_o)

    pl.semaphore_wait(barrier, len(partners))
    to_right = pltpu.make_async_remote_copy(
        gin.at[:, cells - reach1 :], low, halo_send.at[0], halo_recv.at[0], device_id=right, device_id_type=MESH
    )
    to_left = pltpu.make_async_remote_copy(
        gin.at[:, 0:reach1], high, halo_send.at[1], halo_recv.at[1], device_id=left, device_id_type=MESH
    )
    to_right.start()
    to_left.start()
    meet(0, y_peers)

    vec[...] = jnp.zeros_like(vec)
    vec[0:6, :] = fb[...]
    vec[8:13, :] = ng[...]
    vec[16:17, 0 : ob.shape[1]] = ob[...]
    cols[...] = vec[0:128, :].T
    embed[...] = jnp.zeros_like(embed)
    ginx[...] = jnp.zeros_like(ginx)
    sent[:, ext:] = edge_columns(vec, gwt[0], fb[1:2, :])

    copies["we"].wait()
    copies["own"].wait()
    channels = own.shape[0]
    embed[0:channels, :] = w_e[...]

    def embedded(values):
        h = silu(dot_tn(embed[...], values) + cols[:, 0:1]).astype(BF)
        return (normed(dot(w_s[0], h)) * cols[:, 8:9]).astype(BF)

    ginx[0:channels, 0:cells] = own[...]
    copies["s0"].wait()
    copies["g2m"].wait()
    lat[...] = embedded(ginx[:, 0:cells])
    sent[:, 0:cells] = dot(w_g[...], lat[...]).astype(BF)
    pl.semaphore_wait(stage.at[0], 3)
    meet(1, z_peers)

    w = 512
    edges1, edges2 = send1.shape[0], slot.shape[0]
    steps1 = [slice(i * w, (i + 1) * w) for i in range(edges1 // w)]
    steps2 = [slice(i * w, (i + 1) * w) for i in range(edges2 // w)]

    def sender(at):
        v = send1[at].reshape(1, w) - me * cells
        return jnp.where(v < 0, v + ext, v)

    for at in steps1:
        hot = one_hot(sender(at), cells)
        pre3[:, at] = dot(sent[:, 0:cells], hot) + dot(sent[:, ext:], padded(features(geom1[:, at])))

    r = lax.broadcasted_iota(jnp.int32, (1, links), 1) // 16
    dz, dy = r // 4 % 4, r % 4
    dx, dc = (r // 32 + dz + dy) % 4, r // 16 % 2
    to = ((x + dx) % 4 * 2 + (core + dc) % 2) * 16 + (z + dz) % 4 * 4 + (y + dy) % 4
    spread = (lax.broadcasted_iota(jnp.int32, (256, links), 0) == to).astype(BF)
    lists = jnp.concatenate([rows_t[...], jnp.zeros_like(rows_t)], axis=1)
    picked = dot((lists // 16).astype(F32).astype(BF), spread) * 16.0 + dot(
        (lists % 16).astype(F32).astype(BF), spread
    )
    mine = (
        lax.broadcasted_iota(jnp.int32, picked.shape, 0)
        == lax.broadcasted_iota(jnp.int32, picked.shape, 1) % 16
    )
    rows = jnp.sum(jnp.where(mine, picked, 0.0), axis=0, keepdims=True).astype(jnp.int32)

    to_right.wait()
    to_left.wait()
    ginx[0:channels, cells : cells + reach1] = high[...]
    ginx[0:channels, cells + reach1 :] = low[...]
    sent[:, cells:ext] = dot(w_g[...], embedded(ginx[:, cells:])).astype(BF)
    pl.semaphore_wait(stage.at[1], 3)
    meet(2, x_peers)

    copies["s1"].wait()

    def second_layer(k, v):
        return dot(w_s[k], silu(v).astype(BF))

    def pipelined(steps, make, use):
        held = None
        for i in range(len(steps) + 1):
            now = make(steps[i]) if i < len(steps) else None
            if held is not None:
                use(steps[i - 1], held)
            held = now

    acc[...] = jnp.zeros_like(acc)

    def make1(at):
        hot = one_hot(sender(at) - cells, 2 * reach1)
        return second_layer(1, pre3[:, at] + dot(sent[:, cells:ext], hot))

    def use1(at, v):
        acc[...] += dot_nt(normed(v).astype(BF), one_hot(recv1[at].reshape(1, w) - me * nodes, nodes))

    pipelined(steps1, make1, use1)
    ml[...] = (acc[...] * cols[:, 9:10]).astype(BF)
    copies["p00"].wait()
    link = dot_nt(ml[...].astype(F32).T.astype(BF), w_p[0, 0]).astype(BF)
    pl.semaphore_wait(stage.at[2], 3)

    def out_copy(g, k):
        dz, dy = k // 4, k % 4
        to_s = (x + g // 2 + dz + dy) % 4 * 2 + (core + g) % 2
        to_c = (z + dz) % 4 * 4 + (y + dy) % 4
        at = pl.ds(pl.multiple_of((g * 16 + k) * 16, 16), 16)
        return pltpu.make_async_remote_copy(
            outgoing.at[at],
            arrived.at[at],
            a2a_send,
            a2a_recv.at[g],
            device_id=(to_s, to_c),
            device_id_type=MESH,
        )

    order = list(range(1, 8)) + [0]
    for g in order:
        at = slice(g * 256, (g + 1) * 256)
        outgoing[at, :] = dot_tn(one_hot(rows[:, at], nodes), link).astype(BF)

        @pl.loop(0 if g else 1, 16)
        def _(k):
            out_copy(g, k).start()

    arrived[0:16, :] = outgoing[0:16, :]

    copies["p01"].wait()
    own_link = jnp.concatenate(
        [dot(w_p[0, 1], ml[...]).astype(BF), edge_columns(vec, gwt[1], fb[2:3, :])], axis=1
    )

    @pl.loop(0, edges2 // w)
    def _(i):
        at = pl.ds(pl.multiple_of(i * w, w), w)
        hot = one_hot(recv2[at].reshape(1, w) - me * nodes, nodes)
        pre[:, at] = dot(own_link, jnp.concatenate([hot, padded(features(geom2[:, at]))], axis=0))

    copies["p21"].wait()
    copies["p30"].wait()
    outp[...] = dot(w_p[3, 0], lat[...]) + cols[:, 5:6]
    both3 = jnp.concatenate([w_p[2, 1], edge_columns(vec, gwt[2], fb[4:5, :])], axis=1)

    v = send3[...].reshape(1, 3 * cells) - me * nodes
    v = jnp.where(v < 0, v + near3, v)
    feat[...] = features(geom3[...], [(v // 16).astype(F32), (v % 16).astype(F32)])
    wq = 256
    for q in range(cells // wq):
        part = feat[:, q * 3 * wq : (q + 1) * 3 * wq].astype(BF)
        here = lat[:, q * wq : (q + 1) * wq]
        for j in range(3):
            take = (
                lax.broadcasted_iota(jnp.int32, (3 * wq, wq), 0)
                == 3 * lax.broadcasted_iota(jnp.int32, (3 * wq, wq), 1) + j
            ).astype(BF)
            got = dot(part, take)
            at = slice((3 * q + j) * wq, (3 * q + j + 1) * wq)
            send4[:, at] = (got[8:9, :] * 16.0 + got[9:10, :]).astype(jnp.int32)
            pre3[:, at] = dot(both3, jnp.concatenate([here, padded(got[0:8, :])], axis=0))

    t = slot[...].reshape(1, edges2)
    p = t // 16
    dz, dy = (z - p // 4 % 4 + 4) % 4, (y - p % 4 + 4) % 4
    dx, dc = (x - p // 32 + 4) % 4, (core - p // 16 % 2 + 2) % 2
    place = ((((dx - dz - dy + 8) % 4 * 2 + dc) * 4 + dz) * 4 + dy) * 16 + t % 16

    def landed(g):
        got = arrived.at[pl.ds(0, 16 * (16 if g else 15))]
        pltpu.make_async_copy(got, got, a2a_recv.at[g]).wait()

    for pair_of in ((1, 2), (3, 4), (5, 6), (7, 0)):
        block, local = [], []
        for g in pair_of:
            landed(g)
            block.append(arrived[g * 256 : (g + 1) * 256, :])
            local.append(g * 256)
        block = jnp.concatenate(block, axis=0)
        for at in steps2:
            hot = jnp.concatenate([one_hot(place[:, at] - first, 256) for first in local], axis=0)
            pre[:, at] += dot_tn(block, hot)
    gone = outgoing.at[pl.ds(0, 16 * 127)]
    pltpu.make_async_copy(gone, gone, a2a_send).wait()

    acc[...] = jnp.zeros_like(acc)
    copies["s2"].wait()

    def use2(at, v):
        acc[...] += dot_nt(normed(v).astype(BF), one_hot(recv2[at].reshape(1, w) - me * nodes, nodes))

    pipelined(steps2, lambda at: second_layer(2, pre[:, at]), use2)

    for name in ("p10", "p11", "s3", "p20"):
        copies[name].wait()

    def update(latent, total):
        aggregate = (total * cols[:, 10:11]).astype(BF)
        hidden = silu(dot(w_p[1, 0], latent) + dot(w_p[1, 1], aggregate) + cols[:, 3:4]).astype(BF)
        state = (latent.astype(F32) + normed(dot(w_s[3], hidden)) * cols[:, 11:12]).astype(BF)
        return state, dot(w_p[2, 0], state).astype(BF)

    last = nodes - reach3
    both = lambda ref: jnp.concatenate([ref[:, 0:reach3], ref[:, last:]], axis=1)
    state, out = update(both(ml), both(acc))
    state_out[:, 0:reach3] = state[:, 0:reach3]
    state_out[:, last:] = state[:, reach3:]
    ds[:, 0:reach3] = out[:, 0:reach3]
    ds[:, last:nodes] = out[:, reach3:]
    to_right = pltpu.make_async_remote_copy(
        ds.at[:, last:nodes],
        ds.at[:, nodes + reach3 :],
        halo_send.at[2],
        halo_recv.at[2],
        device_id=right,
        device_id_type=MESH,
    )
    to_left = pltpu.make_async_remote_copy(
        ds.at[:, 0:reach3],
        ds.at[:, nodes : nodes + reach3],
        halo_send.at[3],
        halo_recv.at[3],
        device_id=left,
        device_id_type=MESH,
    )
    to_right.start()
    to_left.start()
    state, out = update(ml[:, reach3:last], acc[:, reach3:last])
    state_out[:, reach3:last] = state
    ds[:, reach3:last] = out
    save_state = pltpu.make_async_copy(state_out, state_hbm, out_sem.at[0])
    save_state.start()

    @pl.loop(0, 3 * cells // w)
    def _(i):
        at = pl.ds(pl.multiple_of(i * w, w), w)
        pre3[:, at] += dot(ds[:, 0:nodes], one_hot(send4[:, at], nodes))

    for name in ("s4", "p31", "ow"):
        copies[name].wait()
    to_right.wait()
    to_left.wait()

    outs = ow.shape[0]
    sums = {}

    def make3(step):
        q, j = step
        at = slice((3 * q + j) * wq, (3 * q + j + 1) * wq)
        hot = one_hot(send4[:, at] - nodes, 2 * reach3)
        return second_layer(4, pre3[:, at] + dot(ds[:, nodes:], hot))

    def use3(step, v):
        q, j = step
        message = normed(v).astype(BF).astype(F32)
        sums[q] = sums[q] + message if j else message
        if j == 2:
            at = slice(q * wq, (q + 1) * wq)
            gathered = (sums.pop(q) * cols[:, 12:13]).astype(BF)
            hidden = silu(outp[:, at] + dot(w_p[3, 1], gathered)).astype(BF)
            pred_out[:, at] = dot(w_o[...], hidden) + cols[0:outs, 16:17]

    pipelined([(q, j) for q in range(cells // wq) for j in range(3)], make3, use3)
    save = pltpu.make_async_copy(pred_out, pred_hbm, out_sem.at[1])
    save.start()
    save_state.wait()
    save.wait()


def keep(a, b, a_out, b_out):
    a_out[...] = a[...]
    b_out[...] = b[...]


def body(
    grid_in,
    grid_embed_w,
    g2m_w,
    pair_w,
    second_w,
    first_b,
    norm_gain,
    geom_w,
    out_w,
    out_b,
    g2m_geom,
    mesh_geom,
    m2g_geom,
    g2m_send,
    g2m_recv,
    mesh_recv,
    mesh_slot,
    mesh_rows,
    m2g_send,
):
    width, channels = grid_embed_w.shape
    cells = grid_in.shape[1]
    nodes = 512
    links = mesh_rows.size
    reach = cells // 4
    ext = cells + 2 * reach
    outs = out_w.shape[0]
    args = (
        grid_in,
        grid_embed_w.T,
        g2m_w,
        pair_w,
        second_w,
        first_b,
        norm_gain,
        geom_w.transpose(0, 2, 1),
        out_w,
        out_b.reshape(1, -1),
        g2m_geom,
        mesh_geom,
        m2g_geom,
        g2m_send,
        g2m_recv,
        mesh_recv,
        mesh_slot,
        mesh_rows.T,
        m2g_send,
    )
    hbm, vmem = pl.BlockSpec(memory_space=pl.ANY), pl.BlockSpec(memory_space=pltpu.VMEM)
    in_specs = [vmem] * len(args)
    for k in (0, 1, 2, 3, 4, 8):
        in_specs[k] = hbm
    V = pltpu.VMEM
    shapes = [jax.ShapeDtypeStruct((outs, cells), F32), jax.ShapeDtypeStruct((width, nodes), BF)]
    made = pl.pallas_call(
        kernel,
        in_specs=in_specs,
        out_specs=[hbm, hbm],
        out_shape=shapes,
        scratch_shapes=[
            V((channels, width), BF),
            V((width, width), BF),
            V(pair_w.shape, BF),
            V(second_w.shape, BF),
            V(out_w.shape, BF),
            V((channels, cells), BF),
            V((channels, reach), BF),
            V((channels, reach), BF),
            V((256, ext), BF),
            V((256, width), BF),
            V((256, width), F32),
            V((width, 128), F32),
            V((16, m2g_send.shape[0]), F32),
            V((width, ext + 256), BF),
            V((width, cells), BF),
            V((width, cells), F32),
            V((width, nodes), F32),
            V((width, nodes), BF),
            V((links, width), BF),
            V((links, width), BF),
            V((width, mesh_slot.shape[0]), F32),
            V((width, m2g_send.shape[0]), F32),
            V((width, nodes + nodes // 2), BF),
            V((1, m2g_send.shape[0]), jnp.int32),
            V((outs, cells), F32),
            V((width, nodes), BF),
            pltpu.SemaphoreType.DMA((17,)),
            pltpu.SemaphoreType.DMA((4,)),
            pltpu.SemaphoreType.DMA((4,)),
            pltpu.SemaphoreType.DMA,
            pltpu.SemaphoreType.DMA((8,)),
            pltpu.SemaphoreType.DMA((2,)),
            pltpu.SemaphoreType.REGULAR((3,)),
        ],
        compiler_params=pltpu.CompilerParams(
            collective_id=0, has_side_effects=True, vmem_limit_bytes=60 << 20
        ),
        name="graph",
    )(*args)
    blocks = [pl.BlockSpec((outs, cells // 4), lambda i: (0, i)), pl.BlockSpec((width // 4, nodes), lambda i: (i, 0))]
    return tuple(
        pl.pallas_call(
            keep,
            grid=(4,),
            in_specs=blocks,
            out_specs=blocks,
            out_shape=shapes,
            name="keep",
        )(*made)
    )


def solution(mesh):
    return jax.shard_map(
        body,
        mesh=mesh,
        in_specs=(
            P(None, AXES),
            P(),
            P(),
            P(),
            P(),
            P(),
            P(),
            P(),
            P(),
            P(),
            P(None, AXES),
            P(None, AXES),
            P(None, AXES),
            P(AXES),
            P(AXES),
            P(AXES),
            P(AXES),
            P(AXES, None),
            P(AXES),
        ),
        out_specs=(P(None, AXES), P(None, AXES)),
        check_vma=False,
    )
```

```python
import functools

import jax
import jax.numpy as jnp
from jax import lax
from jax.experimental import pallas as pl
from jax.experimental.pallas import tpu as pltpu
from jax.sharding import PartitionSpec as P

EPS = 1e-05
BF = jnp.bfloat16
F32 = jnp.float32
AXES = ("space", "chan")
MESH = pl.DeviceIdType.MESH


def dot(a, b):
    return lax.dot_general(a, b, (((1,), (0,)), ((), ())), preferred_element_type=F32)


def dot_nt(a, b):
    return lax.dot_general(a, b, (((1,), (1,)), ((), ())), preferred_element_type=F32)


def dot_tn(a, b):
    return lax.dot_general(a, b, (((0,), (0,)), ((), ())), preferred_element_type=F32)


def silu(v):
    u = 0.5 * v
    return u + u * jnp.tanh(u)


def normed(y):
    n = y.shape[0]
    m = jnp.sum(y, axis=0, keepdims=True) * (1.0 / n)
    s = jnp.sum(y * y, axis=0, keepdims=True) * (1.0 / n)
    r = lax.rsqrt(s - m * m + EPS)
    return y * r - m * r


def one_hot(row, n):
    return (lax.broadcasted_iota(jnp.int32, (n, row.shape[1]), 0) == row).astype(BF)


def edge_columns(vec, gwt, bias):
    vec[...] = jnp.zeros_like(vec)
    vec[0:4, :] = gwt.astype(F32)
    for k in range(3):
        head = bias.astype(BF).astype(F32)
        vec[4 + k : 5 + k, :] = head
        bias = bias - head
    return vec[...].T.astype(BF)


def features(geom, extra=()):
    n = geom.shape[1]
    rows = [geom.astype(F32), jnp.ones((3, n), F32), jnp.zeros((1, n), F32)]
    return jnp.concatenate(rows + list(extra) + [jnp.zeros((8 - len(extra), n), F32)], axis=0)


def padded(feats):
    return jnp.concatenate([feats, jnp.zeros((256 - feats.shape[0], feats.shape[1]), F32)], axis=0).astype(BF)


def kernel(
    gin,
    wet,
    g2m,
    pair,
    second,
    fb,
    ng,
    gwt,
    ow,
    ob,
    geom1,
    geom2,
    geom3,
    send1,
    recv1,
    recv2,
    slot,
    rows_t,
    send3,
    pred_hbm,
    state_hbm,
    w_e,
    w_g,
    w_p,
    w_s,
    w_o,
    own,
    low,
    high,
    ginx,
    embed,
    vec,
    cols,
    feat,
    sent,
    lat,
    outp,
    node,
    acc,
    ml,
    outgoing,
    arrived,
    pre,
    pre3,
    ds,
    first_out,
    last_out,
    next_in,
    prev_in,
    send4,
    pred_out,
    state_out,
    w_sem,
    halo_send,
    halo_recv,
    a2a_send,
    a2a_recv,
    out_sem,
    stage,
):
    s, c = lax.axis_index("space"), lax.axis_index("chan")
    me = s * 16 + c
    x, core, z, y = s // 2, s % 2, c // 4, c % 4
    cells, nodes = own.shape[1], ml.shape[1]
    reach1 = low.shape[1]
    reach3 = nodes // 4
    ext = cells + 2 * reach1
    width, links = ml.shape[0], arrived.shape[0]
    near3 = nodes + 2 * reach3

    def flat(d):
        d = (d + 128) % 128
        return (d // 16, d % 16)

    left, right = flat(me - 1), flat(me + 1)
    y_peers = [(s, z * 4 + (y + k) % 4) for k in (1, 2, 3)]
    z_peers = [(s, (z + k) % 4 * 4 + y) for k in (1, 2, 3)]
    x_peers = [((x + k) % 4 * 2 + core, c) for k in (1, 2, 3)]
    partners = [left, right, (x * 2 + 1 - core, c)] + y_peers + z_peers + x_peers
    barrier = pltpu.get_barrier_semaphore()
    for peer in partners:
        pl.semaphore_signal(barrier, inc=1, device_id=peer, device_id_type=MESH)

    def meet(k, peers):
        for peer in peers:
            pl.semaphore_signal(stage.at[k], inc=1, device_id=peer, device_id_type=MESH)

    copies = {}

    def fetch(name, src, dst):
        copies[name] = pltpu.make_async_copy(src, dst, w_sem.at[len(copies)])
        copies[name].start()

    fetch("own", gin, own)
    fetch("we", wet, w_e)
    fetch("s0", second.at[0], w_s.at[0])
    fetch("g2m", g2m, w_g)
    fetch("s1", second.at[1], w_s.at[1])
    fetch("p00", pair.at[0, 0], w_p.at[0, 0])
    fetch("p01", pair.at[0, 1], w_p.at[0, 1])
    fetch("p21", pair.at[2, 1], w_p.at[2, 1])
    fetch("p30", pair.at[3, 0], w_p.at[3, 0])
    fetch("s2", second.at[2], w_s.at[2])
    fetch("p10", pair.at[1, 0], w_p.at[1, 0])
    fetch("p11", pair.at[1, 1], w_p.at[1, 1])
    fetch("s3", second.at[3], w_s.at[3])
    fetch("p20", pair.at[2, 0], w_p.at[2, 0])
    fetch("s4", second.at[4], w_s.at[4])
    fetch("p31", pair.at[3, 1], w_p.at[3, 1])
    fetch("ow", ow, w_o)

    pl.semaphore_wait(barrier, len(partners))
    to_right = pltpu.make_async_remote_copy(
        gin.at[:, cells - reach1 :], low, halo_send.at[0], halo_recv.at[0], device_id=right, device_id_type=MESH
    )
    to_left = pltpu.make_async_remote_copy(
        gin.at[:, 0:reach1], high, halo_send.at[1], halo_recv.at[1], device_id=left, device_id_type=MESH
    )
    to_right.start()
    to_left.start()
    meet(0, y_peers)

    vec[...] = jnp.zeros_like(vec)
    vec[0:6, :] = fb[...]
    vec[8:13, :] = ng[...]
    vec[16:17, 0 : ob.shape[1]] = ob[...]
    cols[...] = vec[0:128, :].T
    channels = own.shape[0]
    pad = channels // 16 * 16
    embed[pad:, :] = jnp.zeros((embed.shape[0] - pad, width), BF)
    ginx[pad:, :] = jnp.zeros((embed.shape[0] - pad, ext), BF)
    sent[:, ext:] = edge_columns(vec, gwt[0], fb[1:2, :])

    copies["we"].wait()
    copies["own"].wait()
    embed[0:channels, :] = w_e[...]

    def embedded(values):
        h = silu(dot_tn(embed[...], values) + cols[:, 0:1]).astype(BF)
        return (normed(dot(w_s[0], h)) * cols[:, 8:9]).astype(BF)

    ginx[0:channels, 0:cells] = own[...]
    copies["s0"].wait()
    copies["g2m"].wait()
    lat[...] = embedded(ginx[:, 0:cells])
    sent[:, 0:cells] = dot(w_g[...], lat[...]).astype(BF)
    pl.semaphore_wait(stage.at[0], 3)
    meet(1, z_peers)

    w = 512
    edges1, edges2 = send1.shape[0], slot.shape[0]
    steps1 = [slice(i * w, (i + 1) * w) for i in range(edges1 // w)]
    steps2 = [slice(i * w, (i + 1) * w) for i in range(edges2 // w)]

    def sender(at):
        v = send1[at].reshape(1, w) - me * cells
        return jnp.where(v < 0, v + ext, v)

    for at in steps1:
        hot = one_hot(sender(at), cells)
        pre3[:, at] = dot(sent[:, 0:cells], hot) + dot(sent[:, ext:], padded(features(geom1[:, at])))

    r = lax.broadcasted_iota(jnp.int32, (1, links), 1) // 16
    dz, dy = r // 4 % 4, r % 4
    dx, dc = (r // 32 + dz + dy) % 4, r // 16 % 2
    to = ((x + dx) % 4 * 2 + (core + dc) % 2) * 16 + (z + dz) % 4 * 4 + (y + dy) % 4
    spread = (lax.broadcasted_iota(jnp.int32, (256, links), 0) == to).astype(BF)
    lists = jnp.concatenate([rows_t[...], jnp.zeros_like(rows_t)], axis=1)
    picked = dot((lists // 16).astype(F32).astype(BF), spread) * 16.0 + dot(
        (lists % 16).astype(F32).astype(BF), spread
    )
    mine = (
        lax.broadcasted_iota(jnp.int32, picked.shape, 0)
        == lax.broadcasted_iota(jnp.int32, picked.shape, 1) % 16
    )
    rows = jnp.sum(jnp.where(mine, picked, 0.0), axis=0, keepdims=True).astype(jnp.int32)

    to_right.wait()
    to_left.wait()
    ginx[0:channels, cells : cells + reach1] = high[...]
    ginx[0:channels, cells + reach1 :] = low[...]
    halves = [slice(cells, cells + reach1), slice(cells + reach1, ext)]
    values = [dot_tn(embed[...], ginx[:, at]) + cols[:, 0:1] for at in halves]
    values = [dot(w_s[0], silu(v).astype(BF)) for v in values]
    values = [(normed(v) * cols[:, 8:9]).astype(BF) for v in values]
    for at, v in zip(halves, values):
        sent[:, at] = dot(w_g[...], v).astype(BF)
    pl.semaphore_wait(stage.at[1], 3)
    meet(2, x_peers)

    copies["s1"].wait()

    def second_layer(k, v):
        return dot(w_s[k], silu(v).astype(BF))

    def pipelined(steps, make, use):
        held = None
        for i in range(len(steps) + 1):
            now = make(steps[i]) if i < len(steps) else None
            if held is not None:
                use(steps[i - 1], held)
            held = now

    acc[...] = jnp.zeros_like(acc)

    def make1(at):
        hot = one_hot(sender(at) - cells, 2 * reach1)
        return second_layer(1, pre3[:, at] + dot(sent[:, cells:ext], hot))

    def use1(at, v):
        acc[...] += dot_nt(normed(v).astype(BF), one_hot(recv1[at].reshape(1, w) - me * nodes, nodes))

    pipelined(steps1, make1, use1)
    ml[...] = (acc[...] * cols[:, 9:10]).astype(BF)
    copies["p00"].wait()
    link = dot_nt(ml[...].astype(F32).T.astype(BF), w_p[0, 0]).astype(BF)
    pl.semaphore_wait(stage.at[2], 3)

    def out_copy(g, k):
        dz, dy = k // 4, k % 4
        to_s = (x + g // 2 + dz + dy) % 4 * 2 + (core + g) % 2
        to_c = (z + dz) % 4 * 4 + (y + dy) % 4
        at = pl.ds(pl.multiple_of((g * 16 + k) * 16, 16), 16)
        return pltpu.make_async_remote_copy(
            outgoing.at[at],
            arrived.at[at],
            a2a_send,
            a2a_recv.at[g],
            device_id=(to_s, to_c),
            device_id_type=MESH,
        )

    order = list(range(1, 8)) + [0]
    for g in order:
        at = slice(g * 256, (g + 1) * 256)
        outgoing[at, :] = dot_tn(one_hot(rows[:, at], nodes), link).astype(BF)

        @pl.loop(0 if g else 1, 16)
        def _(k):
            out_copy(g, k).start()

    arrived[0:16, :] = outgoing[0:16, :]

    copies["p01"].wait()
    own_link = jnp.concatenate(
        [dot(w_p[0, 1], ml[...]).astype(BF), edge_columns(vec, gwt[1], fb[2:3, :])], axis=1
    )

    @pl.loop(0, edges2 // w)
    def _(i):
        at = pl.ds(pl.multiple_of(i * w, w), w)
        hot = one_hot(recv2[at].reshape(1, w) - me * nodes, nodes)
        pre[:, at] = dot(own_link, jnp.concatenate([hot, padded(features(geom2[:, at]))], axis=0))

    for name in ("p21", "p30", "p10"):
        copies[name].wait()
    node[...] = dot(w_p[1, 0], ml[...]) + cols[:, 3:4]
    outp[...] = dot(w_p[3, 0], lat[...]) + cols[:, 5:6]
    both3 = jnp.concatenate([w_p[2, 1], edge_columns(vec, gwt[2], fb[4:5, :])], axis=1)

    v = send3[...].reshape(1, 3 * cells) - me * nodes
    v = jnp.where(v < 0, v + near3, v)
    feat[...] = features(geom3[...], [(v // 16).astype(F32), (v % 16).astype(F32)])
    wq = 256
    for q in range(cells // wq):
        part = feat[:, q * 3 * wq : (q + 1) * 3 * wq].astype(BF)
        here = lat[:, q * wq : (q + 1) * wq]
        for j in range(3):
            take = (
                lax.broadcasted_iota(jnp.int32, (3 * wq, wq), 0)
                == 3 * lax.broadcasted_iota(jnp.int32, (3 * wq, wq), 1) + j
            ).astype(BF)
            got = dot(part, take)
            at = slice((3 * q + j) * wq, (3 * q + j + 1) * wq)
            send4[:, at] = (got[8:9, :] * 16.0 + got[9:10, :]).astype(jnp.int32)
            pre3[:, at] = dot(both3, jnp.concatenate([here, padded(got[0:8, :])], axis=0))

    t = slot[...].reshape(1, edges2)
    p = t // 16
    dz, dy = (z - p // 4 % 4 + 4) % 4, (y - p % 4 + 4) % 4
    dx, dc = (x - p // 32 + 4) % 4, (core - p // 16 % 2 + 2) % 2
    place = ((((dx - dz - dy + 8) % 4 * 2 + dc) * 4 + dz) * 4 + dy) * 16 + t % 16

    def landed(g):
        got = arrived.at[pl.ds(0, 16 * (16 if g else 15))]
        pltpu.make_async_copy(got, got, a2a_recv.at[g]).wait()

    for pair_of in ((1, 2), (3, 4), (5, 6), (7, 0)):
        block, local = [], []
        for g in pair_of:
            landed(g)
            block.append(arrived[g * 256 : (g + 1) * 256, :])
            local.append(g * 256)
        block = jnp.concatenate(block, axis=0)
        for at in steps2:
            hot = jnp.concatenate([one_hot(place[:, at] - first, 256) for first in local], axis=0)
            pre[:, at] += dot_tn(block, hot)
    gone = outgoing.at[pl.ds(0, 16 * 127)]
    pltpu.make_async_copy(gone, gone, a2a_send).wait()

    acc[...] = jnp.zeros_like(acc)
    copies["s2"].wait()

    def use2(at, v):
        acc[...] += dot_nt(normed(v).astype(BF), one_hot(recv2[at].reshape(1, w) - me * nodes, nodes))

    pipelined(steps2, lambda at: second_layer(2, pre[:, at]), use2)

    for name in ("p11", "s3", "p20"):
        copies[name].wait()

    last = nodes - reach3
    both = lambda ref: jnp.concatenate([ref[:, 0:reach3], ref[:, last:]], axis=1)
    middle = lambda ref: ref[:, reach3:last]
    values = [pick(node) + dot(w_p[1, 1], (pick(acc) * cols[:, 10:11]).astype(BF)) for pick in (both, middle)]
    values = [dot(w_s[3], silu(v).astype(BF)) for v in values]

    def states(pick, v):
        return (pick(ml).astype(F32) + normed(v) * cols[:, 11:12]).astype(BF)

    state = states(both, values[0])
    out = dot(w_p[2, 0], state).astype(BF)
    first_out[...] = out[:, 0:reach3]
    last_out[...] = out[:, reach3:]
    to_right = pltpu.make_async_remote_copy(
        last_out, prev_in, halo_send.at[2], halo_recv.at[2], device_id=right, device_id_type=MESH
    )
    to_left = pltpu.make_async_remote_copy(
        first_out, next_in, halo_send.at[3], halo_recv.at[3], device_id=left, device_id_type=MESH
    )
    to_right.start()
    to_left.start()
    state_out[:, 0:reach3] = state[:, 0:reach3]
    state_out[:, last:] = state[:, reach3:]
    ds[:, 0:reach3] = out[:, 0:reach3]
    ds[:, last:] = out[:, reach3:]
    state = states(middle, values[1])
    state_out[:, reach3:last] = state
    ds[:, reach3:last] = dot(w_p[2, 0], state).astype(BF)
    save_state = pltpu.make_async_copy(state_out, state_hbm, out_sem.at[0])
    save_state.start()

    @pl.loop(0, 3 * cells // w)
    def _(i):
        at = pl.ds(pl.multiple_of(i * w, w), w)
        pre3[:, at] += dot(ds[...], one_hot(send4[:, at], nodes))

    for name in ("s4", "p31", "ow"):
        copies[name].wait()
    to_right.wait()
    to_left.wait()

    outs = ow.shape[0]
    near = jnp.concatenate([next_in[...], prev_in[...]], axis=1)
    sums, saves = {}, []

    def make3(step):
        q, j = step
        at = slice((3 * q + j) * wq, (3 * q + j + 1) * wq)
        hot = one_hot(send4[:, at] - nodes, 2 * reach3)
        return second_layer(4, pre3[:, at] + dot(near, hot))

    def use3(step, v):
        q, j = step
        message = normed(v).astype(BF).astype(F32)
        sums[q] = sums[q] + message if j else message
        if j == 2:
            at = slice(q * wq, (q + 1) * wq)
            gathered = (sums.pop(q) * cols[:, 12:13]).astype(BF)
            hidden = silu(outp[:, at] + dot(w_p[3, 1], gathered)).astype(BF)
            pred_out[:, at] = dot(w_o[...], hidden) + cols[0:outs, 16:17]
            saves.append(pltpu.make_async_copy(pred_out.at[:, at], pred_hbm.at[:, at], out_sem.at[1 + q]))
            saves[-1].start()

    pipelined([(q, j) for q in range(cells // wq) for j in range(3)], make3, use3)
    for save in [save_state] + saves:
        save.wait()


def keep(a, b, a_out, b_out):
    a_out[...] = a[...]
    b_out[...] = b[...]


def body(
    grid_in,
    grid_embed_w,
    g2m_w,
    pair_w,
    second_w,
    first_b,
    norm_gain,
    geom_w,
    out_w,
    out_b,
    g2m_geom,
    mesh_geom,
    m2g_geom,
    g2m_send,
    g2m_recv,
    mesh_recv,
    mesh_slot,
    mesh_rows,
    m2g_send,
):
    width, channels = grid_embed_w.shape
    cells = grid_in.shape[1]
    nodes = 512
    links = mesh_rows.size
    reach = cells // 4
    ext = cells + 2 * reach
    outs = out_w.shape[0]
    args = (
        grid_in,
        grid_embed_w.T,
        g2m_w,
        pair_w,
        second_w,
        first_b,
        norm_gain,
        geom_w.transpose(0, 2, 1),
        out_w,
        out_b.reshape(1, -1),
        g2m_geom,
        mesh_geom,
        m2g_geom,
        g2m_send,
        g2m_recv,
        mesh_recv,
        mesh_slot,
        mesh_rows.T,
        m2g_send,
    )
    hbm, vmem = pl.BlockSpec(memory_space=pl.ANY), pl.BlockSpec(memory_space=pltpu.VMEM)
    in_specs = [vmem] * len(args)
    for k in (0, 1, 2, 3, 4, 8):
        in_specs[k] = hbm
    V = pltpu.VMEM
    shapes = [jax.ShapeDtypeStruct((outs, cells), F32), jax.ShapeDtypeStruct((width, nodes), BF)]
    made = pl.pallas_call(
        kernel,
        in_specs=in_specs,
        out_specs=[hbm, hbm],
        out_shape=shapes,
        scratch_shapes=[
            V((channels, width), BF),
            V((width, width), BF),
            V(pair_w.shape, BF),
            V(second_w.shape, BF),
            V(out_w.shape, BF),
            V((channels, cells), BF),
            V((channels, reach), BF),
            V((channels, reach), BF),
            V((256, ext), BF),
            V((256, width), BF),
            V((256, width), F32),
            V((width, 128), F32),
            V((16, m2g_send.shape[0]), F32),
            V((width, ext + 256), BF),
            V((width, cells), BF),
            V((width, cells), F32),
            V((width, nodes), F32),
            V((width, nodes), F32),
            V((width, nodes), BF),
            V((links, width), BF),
            V((links, width), BF),
            V((width, mesh_slot.shape[0]), F32),
            V((width, m2g_send.shape[0]), F32),
            V((width, nodes), BF),
            V((width, nodes // 4), BF),
            V((width, nodes // 4), BF),
            V((width, nodes // 4), BF),
            V((width, nodes // 4), BF),
            V((1, m2g_send.shape[0]), jnp.int32),
            V((outs, cells), F32),
            V((width, nodes), BF),
            pltpu.SemaphoreType.DMA((17,)),
            pltpu.SemaphoreType.DMA((4,)),
            pltpu.SemaphoreType.DMA((4,)),
            pltpu.SemaphoreType.DMA,
            pltpu.SemaphoreType.DMA((8,)),
            pltpu.SemaphoreType.DMA((1 + cells // 256,)),
            pltpu.SemaphoreType.REGULAR((3,)),
        ],
        compiler_params=pltpu.CompilerParams(
            collective_id=0, has_side_effects=True, vmem_limit_bytes=60 << 20
        ),
        name="graph",
    )(*args)
    blocks = [pl.BlockSpec((outs, cells // 2), lambda i: (0, i)), pl.BlockSpec((width // 2, nodes), lambda i: (i, 0))]
    return tuple(
        pl.pallas_call(
            keep,
            grid=(2,),
            in_specs=blocks,
            out_specs=blocks,
            out_shape=shapes,
            name="keep",
        )(*made)
    )


def solution(mesh):
    return jax.shard_map(
        body,
        mesh=mesh,
        in_specs=(
            P(None, AXES),
            P(),
            P(),
            P(),
            P(),
            P(),
            P(),
            P(),
            P(),
            P(),
            P(None, AXES),
            P(None, AXES),
            P(None, AXES),
            P(AXES),
            P(AXES),
            P(AXES),
            P(AXES),
            P(AXES, None),
            P(AXES),
        ),
        out_specs=(P(None, AXES), P(None, AXES)),
        check_vma=False,
    )
```

```python
import functools

import jax
import jax.numpy as jnp
from jax import lax
from jax.experimental import pallas as pl
from jax.experimental.pallas import tpu as pltpu
from jax.sharding import PartitionSpec as P

EPS = 1e-05
BF = jnp.bfloat16
F32 = jnp.float32
AXES = ("space", "chan")
MESH = pl.DeviceIdType.MESH


def dot(a, b):
    return lax.dot_general(a, b, (((1,), (0,)), ((), ())), preferred_element_type=F32)


def dot_nt(a, b):
    return lax.dot_general(a, b, (((1,), (1,)), ((), ())), preferred_element_type=F32)


def dot_tn(a, b):
    return lax.dot_general(a, b, (((0,), (0,)), ((), ())), preferred_element_type=F32)


def silu(v):
    u = 0.5 * v
    return u + u * jnp.tanh(u)


def normed(y):
    n = y.shape[0]
    m = jnp.sum(y, axis=0, keepdims=True) * (1.0 / n)
    s = jnp.sum(y * y, axis=0, keepdims=True) * (1.0 / n)
    r = lax.rsqrt(s - m * m + EPS)
    return y * r - m * r


def one_hot(row, n):
    return (lax.broadcasted_iota(jnp.int32, (n, row.shape[1]), 0) == row).astype(BF)


def edge_columns(vec, gwt, bias):
    vec[...] = jnp.zeros_like(vec)
    vec[0:4, :] = gwt.astype(F32)
    for k in range(3):
        head = bias.astype(BF).astype(F32)
        vec[4 + k : 5 + k, :] = head
        bias = bias - head
    return vec[...].T.astype(BF)


def features(geom, extra=()):
    n = geom.shape[1]
    rows = [geom.astype(F32), jnp.ones((3, n), F32), jnp.zeros((1, n), F32)]
    return jnp.concatenate(rows + list(extra) + [jnp.zeros((8 - len(extra), n), F32)], axis=0)


def padded(feats):
    return jnp.concatenate([feats, jnp.zeros((256 - feats.shape[0], feats.shape[1]), F32)], axis=0).astype(BF)


def kernel(
    gin,
    wet,
    g2m,
    pair,
    second,
    fb_hbm,
    ng_hbm,
    gwt_hbm,
    ow,
    ob_hbm,
    geom1_hbm,
    geom2_hbm,
    geom3_hbm,
    send1_hbm,
    recv1_hbm,
    recv2_hbm,
    slot_hbm,
    rows_t_hbm,
    send3_hbm,
    pred_hbm,
    state_hbm,
    w_e,
    w_g,
    w_p,
    w_s,
    w_o,
    own,
    low,
    high,
    ginx,
    embed,
    vec,
    cols,
    feat,
    sent,
    lat,
    outp,
    node,
    acc,
    ends,
    message,
    ml,
    outgoing,
    arrived,
    pre,
    pre3,
    ds,
    first_out,
    last_out,
    next_in,
    prev_in,
    send4,
    pred_out,
    state_out,
    w_sem,
    halo_send,
    halo_recv,
    a2a_send,
    a2a_recv,
    out_sem,
    stage,
    fb,
    ng,
    gwt,
    ob,
    geom1,
    geom2,
    geom3,
    send1,
    recv1,
    recv2,
    slot,
    rows_t,
    send3,
):
    s, c = lax.axis_index("space"), lax.axis_index("chan")
    me = s * 16 + c
    x, core, z, y = s // 2, s % 2, c // 4, c % 4
    cells, nodes = own.shape[1], ml.shape[1]
    reach1 = low.shape[1]
    reach3 = nodes // 4
    ext = cells + 2 * reach1
    width, links = ml.shape[0], arrived.shape[0]
    near3 = nodes + 2 * reach3

    def flat(d):
        d = (d + 128) % 128
        return (d // 16, d % 16)

    left, right = flat(me - 1), flat(me + 1)
    y_peers = [(s, z * 4 + (y + k) % 4) for k in (1, 2, 3)]
    z_peers = [(s, (z + k) % 4 * 4 + y) for k in (1, 2, 3)]
    x_peers = [((x + k) % 4 * 2 + core, c) for k in (1, 2, 3)]
    partners = [left, right, (x * 2 + 1 - core, c)] + y_peers + z_peers + x_peers
    barrier = pltpu.get_barrier_semaphore()
    for peer in partners:
        pl.semaphore_signal(barrier, inc=1, device_id=peer, device_id_type=MESH)

    def meet(k, peers):
        for peer in peers:
            pl.semaphore_signal(stage.at[k], inc=1, device_id=peer, device_id_type=MESH)

    copies = {}

    def fetch(name, src, dst):
        copies[name] = pltpu.make_async_copy(src, dst, w_sem.at[len(copies)])
        copies[name].start()

    smalls = (
        ("fb", fb_hbm, fb),
        ("ng", ng_hbm, ng),
        ("gwt", gwt_hbm, gwt),
        ("ob", ob_hbm, ob),
        ("geom1", geom1_hbm, geom1),
        ("geom2", geom2_hbm, geom2),
        ("geom3", geom3_hbm, geom3),
        ("send1", send1_hbm, send1),
        ("recv1", recv1_hbm, recv1),
        ("recv2", recv2_hbm, recv2),
        ("slot", slot_hbm, slot),
        ("rows_t", rows_t_hbm, rows_t),
        ("send3", send3_hbm, send3),
    )
    for small in smalls:
        fetch(*small)
    fetch("own", gin, own)
    fetch("we", wet, w_e)
    fetch("s0", second.at[0], w_s.at[0])
    fetch("g2m", g2m, w_g)
    fetch("s1", second.at[1], w_s.at[1])
    fetch("p00", pair.at[0, 0], w_p.at[0, 0])
    fetch("p01", pair.at[0, 1], w_p.at[0, 1])
    fetch("p21", pair.at[2, 1], w_p.at[2, 1])
    fetch("p30", pair.at[3, 0], w_p.at[3, 0])
    fetch("s2", second.at[2], w_s.at[2])
    fetch("p10", pair.at[1, 0], w_p.at[1, 0])
    fetch("p11", pair.at[1, 1], w_p.at[1, 1])
    fetch("s3", second.at[3], w_s.at[3])
    fetch("p20", pair.at[2, 0], w_p.at[2, 0])
    fetch("s4", second.at[4], w_s.at[4])
    fetch("p31", pair.at[3, 1], w_p.at[3, 1])
    fetch("ow", ow, w_o)

    pl.semaphore_wait(barrier, len(partners))
    to_right = pltpu.make_async_remote_copy(
        gin.at[:, cells - reach1 :], low, halo_send.at[0], halo_recv.at[0], device_id=right, device_id_type=MESH
    )
    to_left = pltpu.make_async_remote_copy(
        gin.at[:, 0:reach1], high, halo_send.at[1], halo_recv.at[1], device_id=left, device_id_type=MESH
    )
    to_right.start()
    to_left.start()
    meet(0, y_peers)

    for small in smalls:
        copies[small[0]].wait()

    vec[...] = jnp.zeros_like(vec)
    vec[0:6, :] = fb[...]
    vec[8:13, :] = ng[...]
    vec[16:17, 0 : ob.shape[1]] = ob[...]
    cols[...] = vec[0:128, :].T
    channels = own.shape[0]
    pad = channels // 16 * 16
    embed[pad:, :] = jnp.zeros((embed.shape[0] - pad, width), BF)
    ginx[pad:, :] = jnp.zeros((embed.shape[0] - pad, ext), BF)
    sent[:, ext:] = edge_columns(vec, gwt[0], fb[1:2, :])

    copies["we"].wait()
    copies["own"].wait()
    embed[0:channels, :] = w_e[...]

    def embedded(values):
        h = silu(dot_tn(embed[...], values) + cols[:, 0:1]).astype(BF)
        return (normed(dot(w_s[0], h)) * cols[:, 8:9]).astype(BF)

    ginx[0:channels, 0:cells] = own[...]
    copies["s0"].wait()
    copies["g2m"].wait()
    lat[...] = embedded(ginx[:, 0:cells])
    sent[:, 0:cells] = dot(w_g[...], lat[...]).astype(BF)
    pl.semaphore_wait(stage.at[0], 3)
    meet(1, z_peers)

    w = 512
    edges1, edges2 = send1.shape[0], slot.shape[0]
    steps1 = [slice(i * w, (i + 1) * w) for i in range(edges1 // w)]
    steps2 = [slice(i * w, (i + 1) * w) for i in range(edges2 // w)]

    def sender(at):
        v = send1[at].reshape(1, w) - me * cells
        return jnp.where(v < 0, v + ext, v)

    for at in steps1:
        hot = one_hot(sender(at), cells)
        pre3[:, at] = dot(sent[:, 0:cells], hot) + dot(sent[:, ext:], padded(features(geom1[:, at])))

    r = lax.broadcasted_iota(jnp.int32, (1, links), 1) // 16
    dz, dy = r // 4 % 4, r % 4
    dx, dc = (r // 32 + dz + dy) % 4, r // 16 % 2
    to = ((x + dx) % 4 * 2 + (core + dc) % 2) * 16 + (z + dz) % 4 * 4 + (y + dy) % 4
    spread = (lax.broadcasted_iota(jnp.int32, (256, links), 0) == to).astype(BF)
    lists = jnp.concatenate([rows_t[...], jnp.zeros_like(rows_t)], axis=1)
    picked = dot((lists // 16).astype(F32).astype(BF), spread) * 16.0 + dot(
        (lists % 16).astype(F32).astype(BF), spread
    )
    mine = (
        lax.broadcasted_iota(jnp.int32, picked.shape, 0)
        == lax.broadcasted_iota(jnp.int32, picked.shape, 1) % 16
    )
    rows = jnp.sum(jnp.where(mine, picked, 0.0), axis=0, keepdims=True).astype(jnp.int32)

    to_right.wait()
    to_left.wait()
    ginx[0:channels, cells : cells + reach1] = high[...]
    ginx[0:channels, cells + reach1 :] = low[...]
    halves = [slice(cells, cells + reach1), slice(cells + reach1, ext)]
    values = [dot_tn(embed[...], ginx[:, at]) + cols[:, 0:1] for at in halves]
    values = [dot(w_s[0], silu(v).astype(BF)) for v in values]
    values = [(normed(v) * cols[:, 8:9]).astype(BF) for v in values]
    for at, v in zip(halves, values):
        sent[:, at] = dot(w_g[...], v).astype(BF)
    pl.semaphore_wait(stage.at[1], 3)
    meet(2, x_peers)

    copies["s1"].wait()

    def second_layer(k, v):
        return dot(w_s[k], silu(v).astype(BF))

    def pipelined(steps, make, use):
        held = None
        for i in range(len(steps) + 1):
            now = make(steps[i]) if i < len(steps) else None
            if held is not None:
                use(steps[i - 1], held)
            held = now

    acc[...] = jnp.zeros_like(acc)

    def make1(at):
        hot = one_hot(sender(at) - cells, 2 * reach1)
        return second_layer(1, pre3[:, at] + dot(sent[:, cells:ext], hot))

    def use1(at, v):
        acc[...] += dot_nt(normed(v).astype(BF), one_hot(recv1[at].reshape(1, w) - me * nodes, nodes))

    pipelined(steps1, make1, use1)
    ml[...] = (acc[...] * cols[:, 9:10]).astype(BF)
    copies["p00"].wait()
    link = dot_nt(ml[...].astype(F32).T.astype(BF), w_p[0, 0]).astype(BF)
    pl.semaphore_wait(stage.at[2], 3)

    def out_copy(g, k):
        dz, dy = k // 4, k % 4
        to_s = (x + g // 2 + dz + dy) % 4 * 2 + (core + g) % 2
        to_c = (z + dz) % 4 * 4 + (y + dy) % 4
        at = pl.ds(pl.multiple_of((g * 16 + k) * 16, 16), 16)
        return pltpu.make_async_remote_copy(
            outgoing.at[at],
            arrived.at[at],
            a2a_send,
            a2a_recv.at[g],
            device_id=(to_s, to_c),
            device_id_type=MESH,
        )

    order = list(range(1, 8)) + [0]
    for g in order:
        at = slice(g * 256, (g + 1) * 256)
        outgoing[at, :] = dot_tn(one_hot(rows[:, at], nodes), link).astype(BF)

        @pl.loop(0 if g else 1, 16)
        def _(k):
            out_copy(g, k).start()

    arrived[0:16, :] = outgoing[0:16, :]

    copies["p01"].wait()
    own_link = jnp.concatenate(
        [dot(w_p[0, 1], ml[...]).astype(BF), edge_columns(vec, gwt[1], fb[2:3, :])], axis=1
    )

    @pl.loop(0, edges2 // w)
    def _(i):
        at = pl.ds(pl.multiple_of(i * w, w), w)
        hot = one_hot(recv2[at].reshape(1, w) - me * nodes, nodes)
        pre[:, at] = dot(own_link, jnp.concatenate([hot, padded(features(geom2[:, at]))], axis=0))

    for name in ("p21", "p30", "p10"):
        copies[name].wait()
    node[...] = dot(w_p[1, 0], ml[...]) + cols[:, 3:4]
    outp[...] = dot(w_p[3, 0], lat[...]) + cols[:, 5:6]
    both3 = jnp.concatenate([w_p[2, 1], edge_columns(vec, gwt[2], fb[4:5, :])], axis=1)

    v = send3[...].reshape(1, 3 * cells) - me * nodes
    v = jnp.where(v < 0, v + near3, v)
    feat[...] = features(geom3[...], [(v // 16).astype(F32), (v % 16).astype(F32)])
    wq = 256
    for q in range(cells // wq):
        part = feat[:, q * 3 * wq : (q + 1) * 3 * wq].astype(BF)
        here = lat[:, q * wq : (q + 1) * wq]
        for j in range(3):
            take = (
                lax.broadcasted_iota(jnp.int32, (3 * wq, wq), 0)
                == 3 * lax.broadcasted_iota(jnp.int32, (3 * wq, wq), 1) + j
            ).astype(BF)
            got = dot(part, take)
            at = slice((3 * q + j) * wq, (3 * q + j + 1) * wq)
            send4[:, at] = (got[8:9, :] * 16.0 + got[9:10, :]).astype(jnp.int32)
            pre3[:, at] = dot(both3, jnp.concatenate([here, padded(got[0:8, :])], axis=0))

    t = slot[...].reshape(1, edges2)
    p = t // 16
    dz, dy = (z - p // 4 % 4 + 4) % 4, (y - p % 4 + 4) % 4
    dx, dc = (x - p // 32 + 4) % 4, (core - p // 16 % 2 + 2) % 2
    place = ((((dx - dz - dy + 8) % 4 * 2 + dc) * 4 + dz) * 4 + dy) * 16 + t % 16

    def landed(g):
        got = arrived.at[pl.ds(0, 16 * (16 if g else 15))]
        pltpu.make_async_copy(got, got, a2a_recv.at[g]).wait()

    for group in ((1, 2), (3, 4), (5, 6), (7,)):
        block, local = [], []
        for g in group:
            landed(g)
            block.append(arrived[g * 256 : (g + 1) * 256, :])
            local.append(g * 256)
        block = jnp.concatenate(block, axis=0)
        for at in steps2:
            hot = jnp.concatenate([one_hot(place[:, at] - first, 256) for first in local], axis=0)
            pre[:, at] += dot_tn(block, hot)
    copies["s2"].wait()
    landed(0)
    gone = outgoing.at[pl.ds(0, 16 * 127)]
    pltpu.make_async_copy(gone, gone, a2a_send).wait()

    last = nodes - reach3
    ends[...] = jnp.zeros_like(ends)

    def receiver(at):
        return recv2[at].reshape(1, -1) - me * nodes

    def make2(at):
        return second_layer(2, pre[:, at] + dot_tn(arrived[0:256, :], one_hot(place[:, at], 256)))

    def use2(at, v):
        message[:, at] = normed(v).astype(BF)
        to = receiver(at)
        to = jnp.where(to < reach3, to, jnp.where(to < last, -1, to - (nodes - 2 * reach3)))
        ends[...] += dot_nt(message[:, at], one_hot(to, 2 * reach3))

    pipelined(steps2, make2, use2)

    for name in ("p11", "s3", "p20"):
        copies[name].wait()

    both = lambda ref: jnp.concatenate([ref[:, 0:reach3], ref[:, last:]], axis=1)
    middle = lambda ref: ref[:, reach3:last]

    def update(pick, total):
        v = pick(node) + dot(w_p[1, 1], (total * cols[:, 10:11]).astype(BF))
        v = normed(dot(w_s[3], silu(v).astype(BF)))
        state = (pick(ml).astype(F32) + v * cols[:, 11:12]).astype(BF)
        return state, dot(w_p[2, 0], state).astype(BF)

    state, out = update(both, ends[...])
    first_out[...] = out[:, 0:reach3]
    last_out[...] = out[:, reach3:]
    to_right = pltpu.make_async_remote_copy(
        last_out, prev_in, halo_send.at[2], halo_recv.at[2], device_id=right, device_id_type=MESH
    )
    to_left = pltpu.make_async_remote_copy(
        first_out, next_in, halo_send.at[3], halo_recv.at[3], device_id=left, device_id_type=MESH
    )
    to_right.start()
    to_left.start()
    state_out[:, 0:reach3] = state[:, 0:reach3]
    state_out[:, last:] = state[:, reach3:]
    ds[:, 0:reach3] = out[:, 0:reach3]
    ds[:, last:] = out[:, reach3:]
    total = dot_nt(message[...], one_hot(receiver(slice(0, edges2)) - reach3, last - reach3))
    state, out = update(middle, total)
    state_out[:, reach3:last] = state
    ds[:, reach3:last] = out
    save_state = pltpu.make_async_copy(state_out, state_hbm, out_sem.at[0])
    save_state.start()

    @pl.loop(0, 3 * cells // w)
    def _(i):
        at = pl.ds(pl.multiple_of(i * w, w), w)
        pre3[:, at] += dot(ds[...], one_hot(send4[:, at], nodes))

    for name in ("s4", "p31", "ow"):
        copies[name].wait()
    to_right.wait()
    to_left.wait()

    outs = ow.shape[0]
    near = jnp.concatenate([next_in[...], prev_in[...]], axis=1)
    sums, saves = {}, []

    def make3(step):
        q, j = step
        at = slice((3 * q + j) * wq, (3 * q + j + 1) * wq)
        hot = one_hot(send4[:, at] - nodes, 2 * reach3)
        return second_layer(4, pre3[:, at] + dot(near, hot))

    def use3(step, v):
        q, j = step
        v = normed(v).astype(BF).astype(F32)
        sums[q] = sums[q] + v if j else v
        if j == 2:
            at = slice(q * wq, (q + 1) * wq)
            gathered = (sums.pop(q) * cols[:, 12:13]).astype(BF)
            hidden = silu(outp[:, at] + dot(w_p[3, 1], gathered)).astype(BF)
            pred_out[:, at] = dot(w_o[...], hidden) + cols[0:outs, 16:17]
            saves.append(pltpu.make_async_copy(pred_out.at[:, at], pred_hbm.at[:, at], out_sem.at[1 + q]))
            saves[-1].start()

    pipelined([(q, j) for q in range(cells // wq) for j in range(3)], make3, use3)
    for save in [save_state] + saves:
        save.wait()


def keep(a, b, a_out, b_out):
    a_out[...] = a[...]
    b_out[...] = b[...]


def body(
    grid_in,
    grid_embed_w,
    g2m_w,
    pair_w,
    second_w,
    first_b,
    norm_gain,
    geom_w,
    out_w,
    out_b,
    g2m_geom,
    mesh_geom,
    m2g_geom,
    g2m_send,
    g2m_recv,
    mesh_recv,
    mesh_slot,
    mesh_rows,
    m2g_send,
):
    width, channels = grid_embed_w.shape
    cells = grid_in.shape[1]
    nodes = 512
    links = mesh_rows.size
    reach = cells // 4
    ext = cells + 2 * reach
    outs = out_w.shape[0]
    args = (
        grid_in,
        grid_embed_w.T,
        g2m_w,
        pair_w,
        second_w,
        first_b,
        norm_gain,
        geom_w.transpose(0, 2, 1),
        out_w,
        out_b.reshape(1, -1),
        g2m_geom,
        mesh_geom,
        m2g_geom,
        g2m_send,
        g2m_recv,
        mesh_recv,
        mesh_slot,
        mesh_rows.T,
        m2g_send,
    )
    hbm = pl.BlockSpec(memory_space=pl.ANY)
    V = pltpu.VMEM
    shapes = [jax.ShapeDtypeStruct((outs, cells), F32), jax.ShapeDtypeStruct((width, nodes), BF)]
    made = pl.pallas_call(
        kernel,
        in_specs=[hbm] * len(args),
        out_specs=[hbm, hbm],
        out_shape=shapes,
        scratch_shapes=[
            V((channels, width), BF),
            V((width, width), BF),
            V(pair_w.shape, BF),
            V(second_w.shape, BF),
            V(out_w.shape, BF),
            V((channels, cells), BF),
            V((channels, reach), BF),
            V((channels, reach), BF),
            V((256, ext), BF),
            V((256, width), BF),
            V((256, width), F32),
            V((width, 128), F32),
            V((16, m2g_send.shape[0]), F32),
            V((width, ext + 256), BF),
            V((width, cells), BF),
            V((width, cells), F32),
            V((width, nodes), F32),
            V((width, nodes), F32),
            V((width, nodes // 2), F32),
            V((width, mesh_slot.shape[0]), BF),
            V((width, nodes), BF),
            V((links, width), BF),
            V((links, width), BF),
            V((width, mesh_slot.shape[0]), F32),
            V((width, m2g_send.shape[0]), F32),
            V((width, nodes), BF),
            V((width, nodes // 4), BF),
            V((width, nodes // 4), BF),
            V((width, nodes // 4), BF),
            V((width, nodes // 4), BF),
            V((1, m2g_send.shape[0]), jnp.int32),
            V((outs, cells), F32),
            V((width, nodes), BF),
            pltpu.SemaphoreType.DMA((30,)),
            pltpu.SemaphoreType.DMA((4,)),
            pltpu.SemaphoreType.DMA((4,)),
            pltpu.SemaphoreType.DMA,
            pltpu.SemaphoreType.DMA((8,)),
            pltpu.SemaphoreType.DMA((1 + cells // 256,)),
            pltpu.SemaphoreType.REGULAR((3,)),
        ]
        + [V(a.shape, a.dtype) for a in args[5:8] + args[9:]],
        compiler_params=pltpu.CompilerParams(
            collective_id=0, has_side_effects=True, vmem_limit_bytes=60 << 20
        ),
        name="graph",
    )(*args)
    blocks = [pl.BlockSpec((outs, cells // 2), lambda i: (0, i)), pl.BlockSpec((width // 2, nodes), lambda i: (i, 0))]
    return tuple(
        pl.pallas_call(
            keep,
            grid=(2,),
            in_specs=blocks,
            out_specs=blocks,
            out_shape=shapes,
            name="keep",
        )(*made)
    )


def solution(mesh):
    return jax.shard_map(
        body,
        mesh=mesh,
        in_specs=(
            P(None, AXES),
            P(),
            P(),
            P(),
            P(),
            P(),
            P(),
            P(),
            P(),
            P(),
            P(None, AXES),
            P(None, AXES),
            P(None, AXES),
            P(AXES),
            P(AXES),
            P(AXES),
            P(AXES),
            P(AXES, None),
            P(AXES),
        ),
        out_specs=(P(None, AXES), P(None, AXES)),
        check_vma=False,
    )
```

```python
import functools

import jax
import jax.numpy as jnp
from jax import lax
from jax.experimental import pallas as pl
from jax.experimental.pallas import tpu as pltpu
from jax.sharding import PartitionSpec as P

EPS = 1e-05
BF = jnp.bfloat16
F32 = jnp.float32
AXES = ("space", "chan")
MESH = pl.DeviceIdType.MESH


def dot(a, b):
    return lax.dot_general(a, b, (((1,), (0,)), ((), ())), preferred_element_type=F32)


def dot_nt(a, b):
    return lax.dot_general(a, b, (((1,), (1,)), ((), ())), preferred_element_type=F32)


def dot_tn(a, b):
    return lax.dot_general(a, b, (((0,), (0,)), ((), ())), preferred_element_type=F32)


def silu(v):
    u = 0.5 * v
    return u + u * jnp.tanh(u)


def normed(y):
    n = y.shape[0]
    m = jnp.sum(y, axis=0, keepdims=True) * (1.0 / n)
    s = jnp.sum(y * y, axis=0, keepdims=True) * (1.0 / n)
    r = lax.rsqrt(s - m * m + EPS)
    return y * r - m * r


def one_hot(row, n):
    return (lax.broadcasted_iota(jnp.int32, (n, row.shape[1]), 0) == row).astype(BF)


def edge_columns(vec, gwt, bias):
    vec[...] = jnp.zeros_like(vec)
    vec[0:4, :] = gwt.astype(F32)
    for k in range(3):
        head = bias.astype(BF).astype(F32)
        vec[4 + k : 5 + k, :] = head
        bias = bias - head
    return vec[...].T.astype(BF)


def features(geom, extra=()):
    n = geom.shape[1]
    rows = [geom.astype(F32), jnp.ones((3, n), F32), jnp.zeros((1, n), F32)]
    return jnp.concatenate(rows + list(extra) + [jnp.zeros((8 - len(extra), n), F32)], axis=0)


def padded(feats):
    return jnp.concatenate([feats, jnp.zeros((256 - feats.shape[0], feats.shape[1]), F32)], axis=0).astype(BF)


def kernel(
    gin,
    wet,
    g2m,
    pair,
    second,
    fb_hbm,
    ng_hbm,
    gwt_hbm,
    ow,
    ob_hbm,
    geom1_hbm,
    geom2_hbm,
    geom3_hbm,
    send1_hbm,
    recv1_hbm,
    recv2_hbm,
    slot_hbm,
    rows_t_hbm,
    send3_hbm,
    pred_hbm,
    state_hbm,
    w_e,
    w_g,
    w_p,
    w_s,
    w_o,
    own,
    low,
    high,
    ginx,
    embed,
    vec,
    cols,
    feat,
    sent,
    lat,
    outp,
    node,
    acc,
    ends,
    message,
    ml,
    outgoing,
    arrived,
    pre,
    pre3,
    ds,
    first_out,
    last_out,
    next_in,
    prev_in,
    send4,
    pred_out,
    state_out,
    w_sem,
    halo_send,
    halo_recv,
    a2a_send,
    a2a_recv,
    out_sem,
    stage,
    fb,
    ng,
    gwt,
    ob,
    geom1,
    geom2,
    geom3,
    send1,
    recv1,
    recv2,
    slot,
    rows_t,
    send3,
):
    s, c = lax.axis_index("space"), lax.axis_index("chan")
    me = s * 16 + c
    x, core, z, y = s // 2, s % 2, c // 4, c % 4
    cells, nodes = own.shape[1], ml.shape[1]
    reach1 = low.shape[1]
    reach3 = nodes // 4
    ext = cells + 2 * reach1
    width, links = ml.shape[0], arrived.shape[0]
    near3 = nodes + 2 * reach3

    def flat(d):
        d = (d + 128) % 128
        return (d // 16, d % 16)

    left, right = flat(me - 1), flat(me + 1)
    y_peers = [(s, z * 4 + (y + k) % 4) for k in (1, 2, 3)]
    z_peers = [(s, (z + k) % 4 * 4 + y) for k in (1, 2, 3)]
    x_peers = [((x + k) % 4 * 2 + core, c) for k in (1, 2, 3)]
    partners = [left, right, (x * 2 + 1 - core, c)] + y_peers + z_peers + x_peers
    barrier = pltpu.get_barrier_semaphore()
    for peer in partners:
        pl.semaphore_signal(barrier, inc=1, device_id=peer, device_id_type=MESH)

    def meet(k, peers):
        for peer in peers:
            pl.semaphore_signal(stage.at[k], inc=1, device_id=peer, device_id_type=MESH)

    copies = {}

    def fetch(name, src, dst):
        copies[name] = pltpu.make_async_copy(src, dst, w_sem.at[len(copies)])
        copies[name].start()

    smalls = (
        ("fb", fb_hbm, fb),
        ("ng", ng_hbm, ng),
        ("gwt", gwt_hbm, gwt),
        ("ob", ob_hbm, ob),
        ("geom1", geom1_hbm, geom1),
        ("geom2", geom2_hbm, geom2),
        ("geom3", geom3_hbm, geom3),
        ("send1", send1_hbm, send1),
        ("recv1", recv1_hbm, recv1),
        ("recv2", recv2_hbm, recv2),
        ("slot", slot_hbm, slot),
        ("rows_t", rows_t_hbm, rows_t),
        ("send3", send3_hbm, send3),
    )
    for small in smalls:
        fetch(*small)
    fetch("own", gin, own)
    fetch("we", wet, w_e)
    fetch("s0", second.at[0], w_s.at[0])
    fetch("g2m", g2m, w_g)
    fetch("s1", second.at[1], w_s.at[1])
    fetch("p00", pair.at[0, 0], w_p.at[0, 0])
    fetch("p01", pair.at[0, 1], w_p.at[0, 1])
    fetch("p21", pair.at[2, 1], w_p.at[2, 1])
    fetch("p30", pair.at[3, 0], w_p.at[3, 0])
    fetch("s2", second.at[2], w_s.at[2])
    fetch("p10", pair.at[1, 0], w_p.at[1, 0])
    fetch("p11", pair.at[1, 1], w_p.at[1, 1])
    fetch("s3", second.at[3], w_s.at[3])
    fetch("p20", pair.at[2, 0], w_p.at[2, 0])
    fetch("s4", second.at[4], w_s.at[4])
    fetch("p31", pair.at[3, 1], w_p.at[3, 1])
    fetch("ow", ow, w_o)

    pl.semaphore_wait(barrier, len(partners))
    to_right = pltpu.make_async_remote_copy(
        gin.at[:, cells - reach1 :], low, halo_send.at[0], halo_recv.at[0], device_id=right, device_id_type=MESH
    )
    to_left = pltpu.make_async_remote_copy(
        gin.at[:, 0:reach1], high, halo_send.at[1], halo_recv.at[1], device_id=left, device_id_type=MESH
    )
    to_right.start()
    to_left.start()
    meet(0, y_peers)

    for small in smalls:
        copies[small[0]].wait()

    vec[...] = jnp.zeros_like(vec)
    vec[0:6, :] = fb[...]
    vec[8:13, :] = ng[...]
    vec[16:17, 0 : ob.shape[1]] = ob[...]
    cols[...] = vec[0:128, :].T
    channels = own.shape[0]
    pad = channels // 16 * 16
    embed[pad:, :] = jnp.zeros((embed.shape[0] - pad, width), BF)
    ginx[pad:, :] = jnp.zeros((embed.shape[0] - pad, ext), BF)
    sent[:, ext:] = edge_columns(vec, gwt[0], fb[1:2, :])

    copies["we"].wait()
    copies["own"].wait()
    embed[0:channels, :] = w_e[...]

    def embedded(values):
        h = silu(dot_tn(embed[...], values) + cols[:, 0:1]).astype(BF)
        return (normed(dot(w_s[0], h)) * cols[:, 8:9]).astype(BF)

    ginx[0:channels, 0:cells] = own[...]
    copies["s0"].wait()
    copies["g2m"].wait()
    lat[...] = embedded(ginx[:, 0:cells])
    sent[:, 0:cells] = dot(w_g[...], lat[...]).astype(BF)
    pl.semaphore_wait(stage.at[0], 3)
    meet(1, z_peers)

    w = 512
    edges1, edges2 = send1.shape[0], slot.shape[0]
    steps1 = [slice(i * w, (i + 1) * w) for i in range(edges1 // w)]
    steps2 = [slice(i * w, (i + 1) * w) for i in range(edges2 // w)]

    def sender(at):
        v = send1[at].reshape(1, w) - me * cells
        return jnp.where(v < 0, v + ext, v)

    for at in steps1:
        hot = one_hot(sender(at), cells)
        pre3[:, at] = dot(sent[:, 0:cells], hot) + dot(sent[:, ext:], padded(features(geom1[:, at])))

    r = lax.broadcasted_iota(jnp.int32, (1, links), 1) // 16
    dz, dy = r // 4 % 4, r % 4
    dx, dc = (r // 32 + dz + dy) % 4, r // 16 % 2
    to = ((x + dx) % 4 * 2 + (core + dc) % 2) * 16 + (z + dz) % 4 * 4 + (y + dy) % 4
    spread = (lax.broadcasted_iota(jnp.int32, (256, links), 0) == to).astype(BF)
    lists = jnp.concatenate([rows_t[...], jnp.zeros_like(rows_t)], axis=1)
    picked = dot((lists // 16).astype(F32).astype(BF), spread) * 16.0 + dot(
        (lists % 16).astype(F32).astype(BF), spread
    )
    mine = (
        lax.broadcasted_iota(jnp.int32, picked.shape, 0)
        == lax.broadcasted_iota(jnp.int32, picked.shape, 1) % 16
    )
    rows = jnp.sum(jnp.where(mine, picked, 0.0), axis=0, keepdims=True).astype(jnp.int32)

    to_right.wait()
    to_left.wait()
    ginx[0:channels, cells : cells + reach1] = high[...]
    ginx[0:channels, cells + reach1 :] = low[...]
    halves = [slice(cells, cells + reach1), slice(cells + reach1, ext)]
    values = [dot_tn(embed[...], ginx[:, at]) + cols[:, 0:1] for at in halves]
    values = [dot(w_s[0], silu(v).astype(BF)) for v in values]
    values = [(normed(v) * cols[:, 8:9]).astype(BF) for v in values]
    for at, v in zip(halves, values):
        sent[:, at] = dot(w_g[...], v).astype(BF)
    pl.semaphore_wait(stage.at[1], 3)
    meet(2, x_peers)

    copies["s1"].wait()

    def second_layer(k, v):
        return dot(w_s[k], silu(v).astype(BF))

    def pipelined(steps, make, use):
        held = None
        for i in range(len(steps) + 1):
            now = make(steps[i]) if i < len(steps) else None
            if held is not None:
                use(steps[i - 1], held)
            held = now

    acc[...] = jnp.zeros_like(acc)

    def make1(at):
        hot = one_hot(sender(at) - cells, 2 * reach1)
        return second_layer(1, pre3[:, at] + dot(sent[:, cells:ext], hot))

    def use1(at, v):
        acc[...] += dot_nt(normed(v).astype(BF), one_hot(recv1[at].reshape(1, w) - me * nodes, nodes))

    pipelined(steps1, make1, use1)
    ml[...] = (acc[...] * cols[:, 9:10]).astype(BF)
    copies["p00"].wait()
    link = dot_nt(ml[...].astype(F32).T.astype(BF), w_p[0, 0]).astype(BF)
    pl.semaphore_wait(stage.at[2], 3)

    def out_copy(g, k):
        dz, dy = k // 4, k % 4
        to_s = (x + g // 2 + dz + dy) % 4 * 2 + (core + g) % 2
        to_c = (z + dz) % 4 * 4 + (y + dy) % 4
        at = pl.ds(pl.multiple_of((g * 16 + k) * 16, 16), 16)
        return pltpu.make_async_remote_copy(
            outgoing.at[at],
            arrived.at[at],
            a2a_send,
            a2a_recv.at[g],
            device_id=(to_s, to_c),
            device_id_type=MESH,
        )

    order = list(range(1, 8)) + [0]
    for g in order:
        at = slice(g * 256, (g + 1) * 256)
        outgoing[at, :] = dot_tn(one_hot(rows[:, at], nodes), link).astype(BF)

        @pl.loop(0 if g else 1, 16)
        def _(k):
            out_copy(g, k).start()

    arrived[0:16, :] = outgoing[0:16, :]

    copies["p01"].wait()
    own_link = jnp.concatenate(
        [dot(w_p[0, 1], ml[...]).astype(BF), edge_columns(vec, gwt[1], fb[2:3, :])], axis=1
    )

    @pl.loop(0, edges2 // w)
    def _(i):
        at = pl.ds(pl.multiple_of(i * w, w), w)
        hot = one_hot(recv2[at].reshape(1, w) - me * nodes, nodes)
        pre[:, at] = dot(own_link, jnp.concatenate([hot, padded(features(geom2[:, at]))], axis=0))

    for name in ("p21", "p30", "p10"):
        copies[name].wait()
    node[...] = dot(w_p[1, 0], ml[...]) + cols[:, 3:4]
    outp[...] = dot(w_p[3, 0], lat[...]) + cols[:, 5:6]
    both3 = jnp.concatenate([w_p[2, 1], edge_columns(vec, gwt[2], fb[4:5, :])], axis=1)

    v = send3[...].reshape(1, 3 * cells) - me * nodes
    v = jnp.where(v < 0, v + near3, v)
    feat[...] = features(geom3[...], [(v // 16).astype(F32), (v % 16).astype(F32)])
    wq = 256
    for q in range(cells // wq):
        part = feat[:, q * 3 * wq : (q + 1) * 3 * wq].astype(BF)
        here = lat[:, q * wq : (q + 1) * wq]
        for j in range(3):
            take = (
                lax.broadcasted_iota(jnp.int32, (3 * wq, wq), 0)
                == 3 * lax.broadcasted_iota(jnp.int32, (3 * wq, wq), 1) + j
            ).astype(BF)
            got = dot(part, take)
            at = slice((3 * q + j) * wq, (3 * q + j + 1) * wq)
            send4[:, at] = (got[8:9, :] * 16.0 + got[9:10, :]).astype(jnp.int32)
            pre3[:, at] = dot(both3, jnp.concatenate([here, padded(got[0:8, :])], axis=0))

    t = slot[...].reshape(1, edges2)
    p = t // 16
    dz, dy = (z - p // 4 % 4 + 4) % 4, (y - p % 4 + 4) % 4
    dx, dc = (x - p // 32 + 4) % 4, (core - p // 16 % 2 + 2) % 2
    place = ((((dx - dz - dy + 8) % 4 * 2 + dc) * 4 + dz) * 4 + dy) * 16 + t % 16

    def landed(g):
        got = arrived.at[pl.ds(0, 16 * (16 if g else 15))]
        pltpu.make_async_copy(got, got, a2a_recv.at[g]).wait()

    for group in ((1, 2), (3, 4), (5, 6), (7,)):
        block, local = [], []
        for g in group:
            landed(g)
            block.append(arrived[g * 256 : (g + 1) * 256, :])
            local.append(g * 256)
        block = jnp.concatenate(block, axis=0)
        for at in steps2:
            hot = jnp.concatenate([one_hot(place[:, at] - first, 256) for first in local], axis=0)
            pre[:, at] += dot_tn(block, hot)
    copies["s2"].wait()
    landed(0)
    gone = outgoing.at[pl.ds(0, 16 * 127)]
    pltpu.make_async_copy(gone, gone, a2a_send).wait()

    last = nodes - reach3
    ends[...] = jnp.zeros_like(ends)

    def receiver(at):
        return recv2[at].reshape(1, -1) - me * nodes

    def make2(at):
        return second_layer(2, pre[:, at] + dot_tn(arrived[0:256, :], one_hot(place[:, at], 256)))

    def use2(at, v):
        message[:, at] = normed(v).astype(BF)
        to = receiver(at)
        to = jnp.where(to < reach3, to, jnp.where(to < last, -1, to - (nodes - 2 * reach3)))
        ends[...] += dot_nt(message[:, at], one_hot(to, 2 * reach3))

    pipelined(steps2, make2, use2)

    for name in ("p11", "s3", "p20"):
        copies[name].wait()

    both = lambda ref: jnp.concatenate([ref[:, 0:reach3], ref[:, last:]], axis=1)
    middle = lambda ref: ref[:, reach3:last]

    def update(pick, total):
        v = pick(node) + dot(w_p[1, 1], (total * cols[:, 10:11]).astype(BF))
        v = normed(dot(w_s[3], silu(v).astype(BF)))
        state = (pick(ml).astype(F32) + v * cols[:, 11:12]).astype(BF)
        return state, dot(w_p[2, 0], state).astype(BF)

    state, out = update(both, ends[...])
    first_out[...] = out[:, 0:reach3]
    last_out[...] = out[:, reach3:]
    to_right = pltpu.make_async_remote_copy(
        last_out, prev_in, halo_send.at[2], halo_recv.at[2], device_id=right, device_id_type=MESH
    )
    to_left = pltpu.make_async_remote_copy(
        first_out, next_in, halo_send.at[3], halo_recv.at[3], device_id=left, device_id_type=MESH
    )
    to_right.start()
    to_left.start()
    state_out[:, 0:reach3] = state[:, 0:reach3]
    state_out[:, last:] = state[:, reach3:]
    ds[:, 0:reach3] = out[:, 0:reach3]
    ds[:, last:] = out[:, reach3:]
    total = dot_nt(message[...], one_hot(receiver(slice(0, edges2)) - reach3, last - reach3))
    state, out = update(middle, total)
    state_out[:, reach3:last] = state
    ds[:, reach3:last] = out
    save_state = pltpu.make_async_copy(state_out, state_hbm, out_sem.at[0])
    save_state.start()

    @pl.loop(0, 3)
    def _(i):
        at = pl.ds(pl.multiple_of(i * cells, cells), cells)
        pre3[:, at] += dot(ds[...], one_hot(send4[:, at], nodes))

    for name in ("s4", "p31", "ow"):
        copies[name].wait()
    to_right.wait()
    to_left.wait()

    outs = ow.shape[0]
    near = jnp.concatenate([next_in[...], prev_in[...]], axis=1)
    sums, saves = {}, []

    def make3(step):
        q, j = step
        at = slice((3 * q + j) * wq, (3 * q + j + 1) * wq)
        hot = one_hot(send4[:, at] - nodes, 2 * reach3)
        return second_layer(4, pre3[:, at] + dot(near, hot))

    def use3(step, v):
        q, j = step
        v = normed(v).astype(BF).astype(F32)
        sums[q] = sums[q] + v if j else v
        if j == 2:
            at = slice(q * wq, (q + 1) * wq)
            gathered = (sums.pop(q) * cols[:, 12:13]).astype(BF)
            hidden = silu(outp[:, at] + dot(w_p[3, 1], gathered)).astype(BF)
            pred_out[:, at] = dot(w_o[...], hidden) + cols[0:outs, 16:17]
            saves.append(pltpu.make_async_copy(pred_out.at[:, at], pred_hbm.at[:, at], out_sem.at[1 + q]))
            saves[-1].start()

    pipelined([(q, j) for q in range(cells // wq) for j in range(3)], make3, use3)
    for save in [save_state] + saves:
        save.wait()


def keep(a, b, a_out, b_out):
    a_out[...] = a[...]
    b_out[...] = b[...]


def body(
    grid_in,
    grid_embed_w,
    g2m_w,
    pair_w,
    second_w,
    first_b,
    norm_gain,
    geom_w,
    out_w,
    out_b,
    g2m_geom,
    mesh_geom,
    m2g_geom,
    g2m_send,
    g2m_recv,
    mesh_recv,
    mesh_slot,
    mesh_rows,
    m2g_send,
):
    width, channels = grid_embed_w.shape
    cells = grid_in.shape[1]
    nodes = 512
    links = mesh_rows.size
    reach = cells // 4
    ext = cells + 2 * reach
    outs = out_w.shape[0]
    args = (
        grid_in,
        grid_embed_w.T,
        g2m_w,
        pair_w,
        second_w,
        first_b,
        norm_gain,
        geom_w.transpose(0, 2, 1),
        out_w,
        out_b.reshape(1, -1),
        g2m_geom,
        mesh_geom,
        m2g_geom,
        g2m_send,
        g2m_recv,
        mesh_recv,
        mesh_slot,
        mesh_rows.T,
        m2g_send,
    )
    hbm = pl.BlockSpec(memory_space=pl.ANY)
    V = pltpu.VMEM
    shapes = [jax.ShapeDtypeStruct((outs, cells), F32), jax.ShapeDtypeStruct((width, nodes), BF)]
    made = pl.pallas_call(
        kernel,
        in_specs=[hbm] * len(args),
        out_specs=[hbm, hbm],
        out_shape=shapes,
        scratch_shapes=[
            V((channels, width), BF),
            V((width, width), BF),
            V(pair_w.shape, BF),
            V(second_w.shape, BF),
            V(out_w.shape, BF),
            V((channels, cells), BF),
            V((channels, reach), BF),
            V((channels, reach), BF),
            V((256, ext), BF),
            V((256, width), BF),
            V((256, width), F32),
            V((width, 128), F32),
            V((16, m2g_send.shape[0]), F32),
            V((width, ext + 256), BF),
            V((width, cells), BF),
            V((width, cells), F32),
            V((width, nodes), F32),
            V((width, nodes), F32),
            V((width, nodes // 2), F32),
            V((width, mesh_slot.shape[0]), BF),
            V((width, nodes), BF),
            V((links, width), BF),
            V((links, width), BF),
            V((width, mesh_slot.shape[0]), F32),
            V((width, m2g_send.shape[0]), F32),
            V((width, nodes), BF),
            V((width, nodes // 4), BF),
            V((width, nodes // 4), BF),
            V((width, nodes // 4), BF),
            V((width, nodes // 4), BF),
            V((1, m2g_send.shape[0]), jnp.int32),
            V((outs, cells), F32),
            V((width, nodes), BF),
            pltpu.SemaphoreType.DMA((30,)),
            pltpu.SemaphoreType.DMA((4,)),
            pltpu.SemaphoreType.DMA((4,)),
            pltpu.SemaphoreType.DMA,
            pltpu.SemaphoreType.DMA((8,)),
            pltpu.SemaphoreType.DMA((1 + cells // 256,)),
            pltpu.SemaphoreType.REGULAR((3,)),
        ]
        + [V(a.shape, a.dtype) for a in args[5:8] + args[9:]],
        compiler_params=pltpu.CompilerParams(
            collective_id=0, has_side_effects=True, vmem_limit_bytes=60 << 20
        ),
        name="graph",
    )(*args)
    blocks = [pl.BlockSpec((outs, cells // 2), lambda i: (0, i)), pl.BlockSpec((width // 2, nodes), lambda i: (i, 0))]
    return tuple(
        pl.pallas_call(
            keep,
            grid=(2,),
            in_specs=blocks,
            out_specs=blocks,
            out_shape=shapes,
            name="keep",
        )(*made)
    )


def solution(mesh):
    return jax.shard_map(
        body,
        mesh=mesh,
        in_specs=(
            P(None, AXES),
            P(),
            P(),
            P(),
            P(),
            P(),
            P(),
            P(),
            P(),
            P(),
            P(None, AXES),
            P(None, AXES),
            P(None, AXES),
            P(AXES),
            P(AXES),
            P(AXES),
            P(AXES),
            P(AXES, None),
            P(AXES),
        ),
        out_specs=(P(None, AXES), P(None, AXES)),
        check_vma=False,
    )
```
